32 devices in a mesh: depth: 4 (over z), tile: 8 (over y, x, core).
Axes of the slice: x: 2, y: 2, z: 4, core: 2. Of those that a mesh axis runs over, the one named last changes fastest.
Arguments:
- density: bfloat16 [32, 256, 1024], P('depth', None, 'tile'), may hold values from 0 to 1
- view_zoom: float32 [2], replicated, may hold values from 0.5 to 0.9
- view_shift: float32 [2], replicated, may hold values from 0 to 16
- tf_weights: float32 [2, 4, 8], replicated, may hold values from 0.25 to 2
- perm_order: int32 [2, 4], replicated, may hold values from 0 to 3, each once within a row
Outputs:
- image: float32 [2, 4, 256, 1024], P(None, None, 'depth', 'tile')
The draws below stay inside these ranges and needn't reach their ends.
All inputs are finite; a program needn't handle non-finite values.
Results may differ from the reference program's by a relative error of at most 0.0028.
Values may be sent and summed in bfloat16 or wider, within the bound.
A program may use at most 64 MiB of HBM per device.

```python
import jax
import jax.numpy as jnp
from jax import lax

CZ = 8
CX = 128
NY = 256
VIEWS = 2
BASIS = 8
RADIUS = 8
NZ = 32
NX = 1024
N_DEPTH = 4


def spread_matrix(fine_count, coarse_count, spacing):
    fine_pos = jnp.arange(fine_count, dtype=jnp.float32) / spacing
    coarse_pos = jnp.arange(coarse_count, dtype=jnp.float32)
    return jnp.maximum(0.0, 1.0 - jnp.abs(fine_pos[:, None] - coarse_pos[None, :]))


def draw_density(key, part):
    coarse_key = jax.random.fold_in(key, 7101)
    noise_key = jax.random.fold_in(key, 7102)
    depth_coarse = NZ // 4 + 1
    row_coarse = NY // 16 + 1
    width_coarse = NX // 16 + 1
    coarse = jax.random.uniform(coarse_key, (depth_coarse, row_coarse, width_coarse), jnp.float32)
    width_map = spread_matrix(NX, width_coarse, 16.0)
    row_map = spread_matrix(NY, row_coarse, 16.0)
    depth_map = spread_matrix(NZ, depth_coarse, 4.0)
    smooth = jnp.einsum('abc,xc->abx', coarse, width_map, precision=lax.Precision.HIGHEST)
    smooth = jnp.einsum('abx,yb->ayx', smooth, row_map, precision=lax.Precision.HIGHEST)
    smooth = jnp.einsum('ayx,za->zyx', smooth, depth_map, precision=lax.Precision.HIGHEST)
    noise = jax.random.uniform(noise_key, (NZ, NY, NX), jnp.float32)
    column_sign = 1.0 - 2.0 * (jnp.arange(NX, dtype=jnp.int32) % 2).astype(jnp.float32)
    row_sign = 1.0 - 2.0 * (jnp.arange(NY, dtype=jnp.int32) % 2).astype(jnp.float32)
    stripes = 0.15 * (column_sign[None, None, :] + row_sign[None, :, None]) + 0.15
    field = 0.5 * smooth + 0.2 * noise + stripes
    return jnp.clip(field, 0.0, 1.0).astype(jnp.bfloat16)


def setup_inputs(seed: int = 0) -> dict:
    key_list = jax.random.split(jax.random.key(seed), 6)
    density = draw_density(jax.random.fold_in(key_list[5], 71), 0)
    view_zoom = jnp.clip(jax.random.uniform(key_list[1], (VIEWS,), jnp.float32, 0.5, 0.9), 0.5, 0.9)
    view_shift = jnp.clip(jax.random.uniform(key_list[2], (VIEWS,), jnp.float32, 0.0, 16.0), 0.0, 16.0)
    tf_weights = jnp.clip(jax.random.uniform(key_list[3], (VIEWS, 4, BASIS), jnp.float32, 0.25, 2.0), 0.25, 2.0)
    perm_order = jax.vmap(lambda own: jax.random.permutation(own, N_DEPTH))(jax.random.split(key_list[4], VIEWS)).reshape((VIEWS, N_DEPTH)).astype(jnp.int32)
    return {"density": density, "view_zoom": view_zoom, "view_shift": view_shift, "tf_weights": tf_weights, "perm_order": perm_order}


OCCLUSION_GAIN = 1.5
EXTINCTION = 0.5


def blur_weights(radius):
    offsets = jnp.arange(-radius, radius + 1, dtype=jnp.float32)
    tap_weights = jnp.exp(-offsets * offsets / 72.0)
    return tap_weights / jnp.sum(tap_weights)


def occlusion_of(padded, radius, depth_cells, width_cells):
    tap_weights = blur_weights(radius)
    tap_count = 2 * radius + 1
    row_count = padded.shape[1]
    along_depth = tap_weights[0] * padded[0:depth_cells].astype(jnp.float32)
    for tap_index in range(1, tap_count):
        along_depth = along_depth + tap_weights[tap_index] * padded[tap_index:tap_index + depth_cells].astype(jnp.float32)
    padded_rows = jnp.pad(along_depth, ((0, 0), (radius, radius), (0, 0)))
    along_rows = tap_weights[0] * padded_rows[:, 0:row_count]
    for tap_index in range(1, tap_count):
        along_rows = along_rows + tap_weights[tap_index] * padded_rows[:, tap_index:tap_index + row_count]
    along_width = tap_weights[0] * along_rows[:, :, 0:width_cells]
    for tap_index in range(1, tap_count):
        along_width = along_width + tap_weights[tap_index] * along_rows[:, :, tap_index:tap_index + width_cells]
    return jnp.exp(-OCCLUSION_GAIN * along_width).astype(jnp.bfloat16)


def resample_table(view_zoom, view_shift, row_count):
    pixel_pos = jnp.arange(row_count, dtype=jnp.float32)
    where_at = view_zoom[:, None] * pixel_pos[None, :] + view_shift[:, None]
    cell_pos = jnp.arange(row_count, dtype=jnp.float32)
    interp_table = jnp.maximum(0.0, 1.0 - jnp.abs(where_at[:, :, None] - cell_pos[None, None, :]))
    return interp_table.reshape(-1, row_count).astype(jnp.bfloat16)


def render_slab(slab_density, slab_shade, interp_table, tf_weights, depth_total):
    view_count = tf_weights.shape[0]
    basis_count = tf_weights.shape[2]
    row_count = slab_density.shape[1]
    width_cells = slab_density.shape[2]

    def one_slice(state_pair, cell_pair):
        colour, passing = state_pair
        density_rows, shade_rows = cell_pair
        stacked = jnp.concatenate([density_rows, shade_rows], axis=1)
        sampled = jnp.dot(interp_table, stacked, preferred_element_type=jnp.float32)
        sampled = sampled.reshape(view_count, row_count, 2 * width_cells)
        sampled_density = sampled[:, :, :width_cells]
        sampled_shade = sampled[:, :, width_cells:]
        values = jnp.zeros((view_count, 4, row_count, width_cells), jnp.float32)
        for basis_index in range(basis_count):
            offset = sampled_density * (basis_count - 1) - basis_index
            bump_value = jnp.exp(-0.5 * offset * offset)
            values = values + tf_weights[:, :, basis_index][:, :, None, None] * bump_value[:, None]
        opacity = 1.0 - jnp.exp(-(EXTINCTION / depth_total) * values[:, 3])
        lit_part = sampled_shade * opacity
        emitted = jnp.concatenate([values[:, 0:3] * lit_part[:, None], opacity[:, None]], axis=1)
        colour = colour + passing[:, None] * emitted
        passing = passing * (1.0 - opacity)
        return (colour, passing), None

    initial = (jnp.zeros((view_count, 4, row_count, width_cells), jnp.float32),
               jnp.ones((view_count, row_count, width_cells), jnp.float32))
    final_state, _ = lax.scan(one_slice, initial, (slab_density, slab_shade))
    return final_state[0].astype(jnp.bfloat16)


def composite(slab_stack, perm_order):
    slab_count = slab_stack.shape[0]
    view_count = slab_stack.shape[1]
    pictures = []
    for view_index in range(view_count):
        per_view = slab_stack[:, view_index]

        def place(state_pair, position):
            picture, passing = state_pair
            chosen = perm_order[view_index, position].astype(jnp.int32)
            slab_now = lax.dynamic_index_in_dim(per_view, chosen, 0, keepdims=False).astype(jnp.float32)
            picture = picture + passing[None] * slab_now
            passing = passing * (1.0 - slab_now[3])
            return (picture, passing), None

        initial = (jnp.zeros(per_view.shape[1:], jnp.float32), jnp.ones(per_view.shape[2:], jnp.float32))
        final_state, _ = lax.scan(place, initial, jnp.arange(slab_count, dtype=jnp.int32))
        pictures.append(final_state[0])
    return jnp.stack(pictures)


def reference(density, view_zoom, view_shift, tf_weights, perm_order):
    slab_count = NZ // CZ
    interp_table = resample_table(view_zoom, view_shift, NY)
    padded = jnp.pad(density, ((RADIUS, RADIUS), (0, 0), (RADIUS, RADIUS)))

    def render_pair(cell_pair):
        return render_slab(cell_pair[0], cell_pair[1], interp_table, tf_weights, NZ)

    def one_tile(tile_index):
        first_column = (tile_index * CX).astype(jnp.int32)
        region = lax.dynamic_slice_in_dim(padded, first_column, CX + 2 * RADIUS, 2)
        shade = occlusion_of(region, RADIUS, NZ, CX)
        tile_density = lax.dynamic_slice_in_dim(density, first_column, CX, 2)
        slab_stack = lax.map(render_pair, (tile_density.reshape(slab_count, CZ, NY, CX),
                                           shade.reshape(slab_count, CZ, NY, CX)))
        return composite(slab_stack, perm_order)

    tile_images = lax.map(one_tile, jnp.arange(NX // CX, dtype=jnp.int32))
    return jnp.transpose(tile_images, (1, 2, 3, 0, 4)).reshape(VIEWS, 4, NY, NX)
```

```python
import functools
import math

import jax
import jax.numpy as jnp
import numpy as np
from jax import lax
from jax.experimental import pallas as pl
from jax.experimental.pallas import tpu as pltpu
from jax.sharding import PartitionSpec as P

RADIUS = 8
OCCLUSION_GAIN = 1.5
EXTINCTION = 0.5
LOG2E = math.log2(math.e)
GROUP = 16
CHUNK = 32


def rounded_taps():
    offsets = np.arange(-RADIUS, RADIUS + 1, dtype=np.float64)
    taps = np.exp(-offsets * offsets / 72.0)
    taps = (taps / taps.sum()).astype(jnp.bfloat16).astype(np.float64)
    return taps, float(taps.sum())


def band(out_count, in_count, shift, taps):
    offset = np.arange(in_count)[None, :] + shift - np.arange(out_count)[:, None]
    inside = np.abs(offset) <= RADIUS
    return np.where(inside, taps[np.clip(offset + RADIUS, 0, 2 * RADIUS)], 0.0)


def constants(cells, rows, width):
    taps, total = rounded_taps()
    pack = np.zeros((cells, width, width), np.float32)
    low = np.zeros((width, cells, width))
    high = np.zeros((width, cells, width))
    half = cells * RADIUS
    from_low = band(width, RADIUS, -RADIUS, taps).T
    from_high = band(width, RADIUS, width, taps).T
    for z in range(cells):
        for j in range(RADIUS):
            pack[z, j, z * RADIUS + j] = 1.0
            pack[z, width - RADIUS + j, half + z * RADIUS + j] = 1.0
        low[half + z * RADIUS : half + (z + 1) * RADIUS, z] = from_low
        high[z * RADIUS : (z + 1) * RADIUS, z] = from_high
    halo = (low + high).reshape(width, cells * width)
    depth = np.kron(band(cells, 3 * cells, -cells, taps), np.eye(GROUP))
    arrays = (
        pack.reshape(cells * width, width),
        band(width, width, 0, taps).T,
        halo,
        band(rows, rows, 0, taps),
        depth,
    )
    return [jnp.asarray(a.astype(jnp.bfloat16)) for a in arrays], total


def matmul(a, b):
    return jnp.dot(a, b, preferred_element_type=jnp.float32)


def kernel(
    slabs, tiles, tap_total,
    density_in, zoom, shift, weights, order, pack_in, width_in, halo_in, height_in, depth_in,
    image_out,
    density, pack_m, width_m, halo_m, height_m, depth_m,
    table, packed, from_left, from_right, edges, edges_low, edges_high,
    plane, plane_low, plane_high, from_low, from_high, sampled, lit, shade, alpha, slab, recv_alpha, image, *rest,
):
    views, channels, basis = weights.shape
    cells, rows, width = density_in.shape
    recv = rest[:views]
    fetch_sem, out_sem, tile_send, tile_recv, depth_send, depth_recv, edge_send, edge_recv, alpha_send, alpha_recv, slab_send, slab_recv = rest[views:]
    group_rows = rows // slabs
    d = lax.axis_index("depth")
    t = lax.axis_index("tile")
    bf16 = jnp.bfloat16

    barrier = pltpu.get_barrier_semaphore()

    def greet(peer):
        pl.semaphore_signal(barrier, inc=1, device_id=peer, device_id_type=pl.DeviceIdType.MESH)

    for j in range(slabs):
        @pl.when(j != d)
        def _():
            greet({"depth": j})

    @pl.when(t > 0)
    def _():
        greet({"tile": t - 1})

    @pl.when(t < tiles - 1)
    def _():
        greet({"tile": t + 1})

    sources = (density_in, pack_in, width_in, halo_in, height_in, depth_in)
    places = (density, pack_m, width_m, halo_m, height_m, depth_m)
    fetches = [
        pltpu.make_async_copy(src, dst, fetch_sem.at[i]) for i, (src, dst) in enumerate(zip(sources, places))
    ]
    for fetch in fetches:
        fetch.start()
    fetches[0].wait()
    fetches[1].wait()

    def remote(src, dst, send, recv_sem, peer):
        return pltpu.make_async_remote_copy(
            src_ref=src, dst_ref=dst, send_sem=send, recv_sem=recv_sem,
            device_id=peer, device_id_type=pl.DeviceIdType.MESH,
        )

    whole = jnp.concatenate([density[z] for z in range(cells)], axis=1)
    packed[...] = matmul(whole, pack_m[...]).astype(bf16)
    to_left = remote(packed, from_right, tile_send.at[0], tile_recv.at[1], {"tile": t - 1})
    to_right = remote(packed, from_left, tile_send.at[1], tile_recv.at[0], {"tile": t + 1})

    pl.semaphore_wait(
        barrier, slabs - 1 + (t > 0).astype(jnp.int32) + (t < tiles - 1).astype(jnp.int32)
    )

    half = cells // 2
    parts = [slice(0, half), slice(half, cells)]
    to_below = [
        remote(density.at[p], from_high.at[p], depth_send.at[0, i], depth_recv.at[1, i], {"depth": d - 1})
        for i, p in enumerate(parts)
    ]
    to_above = [
        remote(density.at[p], from_low.at[p], depth_send.at[1, i], depth_recv.at[0, i], {"depth": d + 1})
        for i, p in enumerate(parts)
    ]

    @pl.when(t > 0)
    def _():
        to_left.start()

    @pl.when(t < tiles - 1)
    def _():
        to_right.start()

    @pl.when(d > 0)
    def _():
        to_below[0].start()

    @pl.when(d < slabs - 1)
    def _():
        to_above[0].start()

    @pl.when(t == 0)
    def _():
        from_left[...] = jnp.zeros_like(from_left)

    @pl.when(t == tiles - 1)
    def _():
        from_right[...] = jnp.zeros_like(from_right)

    @pl.when(d == 0)
    def _():
        from_low[...] = jnp.zeros_like(from_low)
        edges_low[...] = jnp.zeros_like(edges_low)

    @pl.when(d == slabs - 1)
    def _():
        from_high[...] = jnp.zeros_like(from_high)
        edges_high[...] = jnp.zeros_like(edges_high)

    pixel = lax.broadcasted_iota(jnp.int32, (rows, rows), 0).astype(jnp.float32)
    cell = lax.broadcasted_iota(jnp.int32, (rows, rows), 1).astype(jnp.float32)
    for v in range(views):
        where_at = zoom[v] * pixel + shift[v]
        table[v * rows : (v + 1) * rows] = jnp.maximum(0.0, 1.0 - jnp.abs(where_at - cell)).astype(bf16)

    def resample(source, v):
        at = slice(v * rows, (v + 1) * rows)
        for z in range(0, cells, 2):
            pair = matmul(table[at], jnp.concatenate([source[z], source[z + 1]], axis=1))
            sampled[z, at] = pair[:, :width]
            sampled[z + 1, at] = pair[:, width:]

    for v in range(views):
        resample(density, v)
    for fetch in fetches[2:]:
        fetch.wait()

    @pl.when(t > 0)
    def _():
        to_left.wait_send()
        to_right.wait_recv()

    @pl.when(t < tiles - 1)
    def _():
        to_right.wait_send()
        to_left.wait_recv()

    lane = lax.broadcasted_iota(jnp.int32, (rows, width), 1)
    edges[...] = jnp.where(
        lane < cells * RADIUS, from_right[...].astype(jnp.float32), from_left[...].astype(jnp.float32)
    ).astype(bf16)

    def blur_plane(block, sides, out, part):
        count = part.stop - part.start
        inner = matmul(block[part].reshape(count * rows, width), width_m[...])
        outer = matmul(sides[...], halo_m[:, part.start * width : part.stop * width])
        along_width = jnp.concatenate(
            [inner[z * rows : (z + 1) * rows] + outer[:, z * width : (z + 1) * width] for z in range(count)],
            axis=1,
        ).astype(bf16)
        flat = matmul(height_m[...], along_width).astype(bf16)
        for z in range(count):
            out[part.start + z] = flat[:, z * width : (z + 1) * width]

    edges_below = remote(edges, edges_high, edge_send.at[0], edge_recv.at[1], {"depth": d - 1})
    edges_above = remote(edges, edges_low, edge_send.at[1], edge_recv.at[0], {"depth": d + 1})

    @pl.when(d > 0)
    def _():
        edges_below.start()
        to_below[1].start()

    @pl.when(d < slabs - 1)
    def _():
        edges_above.start()
        to_above[1].start()

    blur_plane(density, edges, plane, slice(0, cells))

    chunk = min(CHUNK, group_rows)
    per_group = group_rows // chunk
    extinction = -(EXTINCTION / (cells * slabs)) * LOG2E
    peak = basis - 1
    for v in range(views):
        coef = [
            [
                weights[v, c, k] * (math.exp(-0.5 * k * k) * (extinction if c == channels - 1 else 1.0))
                for k in range(basis)
            ]
            for c in range(channels)
        ]

        def transfer(i, carry, v=v, coef=coef):
            first = pl.multiple_of(i * chunk, chunk)
            passing = jnp.ones((chunk, width), jnp.float32)
            for z in range(cells):
                s = sampled[z, pl.ds(v * rows + first, chunk), :]
                fall = jnp.exp2((-0.5 * peak * peak * LOG2E) * (s * s))
                ratio = jnp.exp2((peak * LOG2E) * s)
                sums = []
                for c in range(channels):
                    total = coef[c][basis - 1] * ratio + coef[c][basis - 2]
                    for k in range(basis - 3, -1, -1):
                        total = total * ratio + coef[c][k]
                    sums.append(total)
                later = passing * jnp.exp2(fall * sums[-1])
                share = (passing - later) * fall
                for c in range(channels - 1):
                    lit[v, c, z, pl.ds(first, chunk), :] = share * sums[c]
                passing = later
            group = i // per_group
            inside = pl.multiple_of((i % per_group) * chunk, chunk)
            alpha[group, v, pl.ds(inside, chunk), :] = (1.0 - passing).astype(bf16)
            return carry

        lax.fori_loop(0, rows // chunk, transfer, 0)

    def peer_of(k):
        return lax.rem(d + k, slabs)

    def alpha_copy(k):
        return remote(alpha.at[peer_of(k)], recv_alpha.at[d], alpha_send.at[k], alpha_recv.at[d], {"depth": peer_of(k)})

    others = sorted(range(1, slabs), key=lambda k: abs(2 * k - slabs))
    for k in others:
        alpha_copy(k).start()
    recv_alpha[d] = alpha[d]

    for i, part in enumerate(parts):
        @pl.when(d > 0)
        def _():
            to_below[i].wait_send()
            to_above[i].wait_recv()
            if i == 0:
                edges_below.wait_send()
                edges_above.wait_recv()

        @pl.when(d < slabs - 1)
        def _():
            to_above[i].wait_send()
            to_below[i].wait_recv()
            if i == 0:
                edges_above.wait_send()
                edges_below.wait_recv()

        blur_plane(from_low, edges_low, plane_low, part)
        blur_plane(from_high, edges_high, plane_high, part)

    gain = -OCCLUSION_GAIN * LOG2E / tap_total**3
    for g in range(0, rows, 2 * GROUP):
        def column(at):
            part = pl.ds(at, GROUP)
            return jnp.concatenate(
                [ref[:, part, :].reshape(cells * GROUP, width) for ref in (plane_low, plane, plane_high)], axis=0
            )

        both = matmul(depth_m[...], jnp.concatenate([column(g), column(g + GROUP)], axis=1))
        both = jnp.exp2(gain * both).astype(bf16)
        shade[:, g : g + GROUP, :] = both[:, :width].reshape(cells, GROUP, width)
        shade[:, g + GROUP : g + 2 * GROUP, :] = both[:, width:].reshape(cells, GROUP, width)

    def slab_copy(v, k):
        return remote(
            slab.at[v, k], recv[v].at[d], slab_send.at[v, k], slab_recv.at[v, d], {"depth": peer_of(k)}
        )

    for v in range(views):
        resample(shade, v)
        for k in others + [0]:
            start = pl.multiple_of(peer_of(k) * group_rows, group_rows)
            for i in range(per_group):
                colour = [jnp.zeros((chunk, width), jnp.float32)] * (channels - 1)
                for z in range(cells):
                    s = sampled[z, pl.ds(v * rows + start + i * chunk, chunk), :]
                    colour = [
                        colour[c] + lit[v, c, z, pl.ds(start + i * chunk, chunk), :] * s
                        for c in range(channels - 1)
                    ]
                for c in range(channels - 1):
                    tint = colour[c].astype(bf16)
                    if k:
                        slab[v, k, c, i * chunk : (i + 1) * chunk, :] = tint
                    else:
                        recv[v][d, c, i * chunk : (i + 1) * chunk, :] = tint
            if k:
                slab_copy(v, k).start()

    for k in others:
        peer = peer_of(k)
        alpha_copy(k).wait_send()
        remote(
            alpha.at[peer], recv_alpha.at[peer], alpha_send.at[k], alpha_recv.at[peer], {"depth": peer}
        ).wait_recv()
    for v in range(views):
        for k in others:
            peer = peer_of(k)
            slab_copy(v, k).wait_send()
            remote(
                slab.at[v, k], recv[v].at[peer], slab_send.at[v, k], slab_recv.at[v, peer], {"depth": peer}
            ).wait_recv()

        picture = jnp.zeros((channels - 1, group_rows, width), jnp.float32)
        cover = jnp.zeros((group_rows, width), jnp.float32)
        passing = jnp.ones((group_rows, width), jnp.float32)
        for q in range(slabs):
            slot = order[v, q]
            dense = recv_alpha[slot, v].astype(jnp.float32)
            picture = picture + passing[None] * recv[v][slot].astype(jnp.float32)
            cover = cover + passing * dense
            passing = passing * (1.0 - dense)
        image_out[v, : channels - 1] = picture
        image_out[v, channels - 1] = cover


def local(slabs, tiles, density, view_zoom, view_shift, tf_weights, perm_order):
    cells, rows, width = density.shape
    views, channels, _ = tf_weights.shape
    group_rows = rows // slabs
    matrices, tap_total = constants(cells, rows, width)
    hbm = pl.BlockSpec(memory_space=pltpu.HBM)
    smem = pl.BlockSpec(memory_space=pltpu.SMEM)
    bf16 = jnp.bfloat16
    block = pltpu.VMEM((cells, rows, width), bf16)
    edge = pltpu.VMEM((rows, width), bf16)
    dma = pltpu.SemaphoreType.DMA
    return pl.pallas_call(
        functools.partial(kernel, slabs, tiles, tap_total),
        out_shape=pltpu.VMEM((views, channels, group_rows, width), jnp.float32),
        in_specs=[hbm, smem, smem, smem, smem] + [hbm] * len(matrices),
        out_specs=pl.BlockSpec(memory_space=pltpu.VMEM),
        scratch_shapes=[block]
        + [pltpu.VMEM(m.shape, bf16) for m in matrices]
        + [
            pltpu.VMEM((views * rows, rows), bf16),
            edge, edge, edge, edge, edge, edge,
            block, block, block, block, block,
            pltpu.VMEM((cells, views * rows, width), jnp.float32),
            pltpu.VMEM((views, channels - 1, cells, rows, width), jnp.float32),
            block,
            pltpu.VMEM((slabs, views, group_rows, width), bf16),
            pltpu.VMEM((views, slabs, channels - 1, group_rows, width), bf16),
            pltpu.VMEM((slabs, views, group_rows, width), bf16),
            pltpu.VMEM((views, channels, group_rows, width), jnp.float32),
        ]
        + [pltpu.VMEM((slabs, channels - 1, group_rows, width), bf16)] * views
        + [dma((1 + len(matrices),)), dma((views,)), dma((2,)), dma((2,)), dma((2, 2)), dma((2, 2)), dma((2,)), dma((2,))]
        + [dma((slabs,)), dma((slabs,))]
        + [dma((views, slabs)), dma((views, slabs))],
        compiler_params=pltpu.CompilerParams(
            collective_id=0, has_side_effects=True, vmem_limit_bytes=40 * 1024 * 1024
        ),
    )(*[pltpu.with_memory_space_constraint(a, pltpu.HBM) for a in (density, view_zoom, view_shift, tf_weights, perm_order, *matrices)])


def solution(mesh):
    placed = (P("depth", None, "tile"), P(), P(), P(), P())
    return jax.shard_map(
        functools.partial(local, mesh.shape["depth"], mesh.shape["tile"]),
        mesh=mesh, in_specs=placed, out_specs=P(None, None, "depth", "tile"), check_vma=False,
    )
```

```python
import functools
import math

import jax
import jax.numpy as jnp
import numpy as np
from jax import lax
from jax.experimental import pallas as pl
from jax.experimental.pallas import tpu as pltpu
from jax.sharding import PartitionSpec as P

RADIUS = 8
OCCLUSION_GAIN = 1.5
EXTINCTION = 0.5
LOG2E = math.log2(math.e)
GROUP = 16
CHUNK = 32
CUTS = (0, 2, 4, 6)
CUTS_OF = 8


def rounded_taps():
    offsets = np.arange(-RADIUS, RADIUS + 1, dtype=np.float64)
    taps = np.exp(-offsets * offsets / 72.0)
    taps = (taps / taps.sum()).astype(jnp.bfloat16).astype(np.float64)
    return taps, float(taps.sum())


def band(out_count, in_count, shift, taps):
    offset = np.arange(in_count)[None, :] + shift - np.arange(out_count)[:, None]
    inside = np.abs(offset) <= RADIUS
    return np.where(inside, taps[np.clip(offset + RADIUS, 0, 2 * RADIUS)], 0.0)


def constants(cells, rows, width):
    taps, total = rounded_taps()
    pack = np.zeros((cells, width, width), np.float32)
    low = np.zeros((width, cells, width))
    high = np.zeros((width, cells, width))
    half = cells * RADIUS
    from_low = band(width, RADIUS, -RADIUS, taps).T
    from_high = band(width, RADIUS, width, taps).T
    for z in range(cells):
        for j in range(RADIUS):
            pack[z, j, z * RADIUS + j] = 1.0
            pack[z, width - RADIUS + j, half + z * RADIUS + j] = 1.0
        low[half + z * RADIUS : half + (z + 1) * RADIUS, z] = from_low
        high[z * RADIUS : (z + 1) * RADIUS, z] = from_high
    halo = (low + high).reshape(width, cells * width)
    depth = np.stack([np.kron(band(cells, 3 * cells, -s * cells, taps), np.eye(GROUP)) for s in (0, 1, 2)])
    arrays = (
        pack.reshape(cells * width, width),
        band(width, width, 0, taps).T,
        halo,
        band(rows, rows, 0, taps),
        depth,
    )
    return [jnp.asarray(a.astype(jnp.bfloat16)) for a in arrays], total


def matmul(a, b):
    return jnp.dot(a, b, preferred_element_type=jnp.float32)


def kernel(
    slabs, tiles, tap_total,
    density_in, zoom, shift, weights, order, pack_in, width_in, halo_in, height_in, depth_in,
    image,
    density, pack_m, width_m, halo_m, height_m, depth_m,
    table, packed, from_left, from_right, edges, edges_side,
    planes, from_side, sampled, sampled_outer, sampled_inner, lit, lit_outer, shade, shade_outer,
    mixing, passing_outer, power_inner, alpha, slab, own, extra, recv_extra, *rest,
):
    views, channels, basis = weights.shape
    cells, rows, width = density_in.shape
    recv = rest[:views]
    (
        fetch_sem, tile_send, tile_recv, depth_send, depth_recv, edge_send, edge_recv,
        alpha_send, alpha_recv, slab_send, slab_recv, extra_send, extra_recv, ready,
    ) = rest[views:]
    group_rows = rows // slabs
    d = lax.axis_index("depth")
    t = lax.axis_index("tile")
    bf16 = jnp.bfloat16
    LOW, HIGH = 0, 1
    colours = channels - 1

    renders = (d > 0) & (d < slabs - 1)
    has_outer = (d == 1) | (d == slabs - 2)
    between = (d > 1) & (d < slabs - 2)
    at_end = (d == 0) | (d == slabs - 1)
    outer_side = jnp.where(d == 1, LOW, HIGH)
    outer = jnp.where(d == 1, 0, slabs - 1)
    inner_side = 1 - outer_side
    inner = jnp.where(d == 1, 2, d - 1)
    step = jnp.where(2 * d < slabs, 1, slabs - 1)

    barrier = pltpu.get_barrier_semaphore()

    def signal(sem, peer):
        pl.semaphore_signal(sem, inc=1, device_id=peer, device_id_type=pl.DeviceIdType.MESH)

    @pl.when(d > 0)
    def _():
        signal(barrier, {"depth": d - 1})

    @pl.when(d < slabs - 1)
    def _():
        signal(barrier, {"depth": d + 1})

    @pl.when(t > 0)
    def _():
        signal(barrier, {"tile": t - 1})

    @pl.when(t < tiles - 1)
    def _():
        signal(barrier, {"tile": t + 1})

    sources = (density_in, pack_in, width_in, halo_in, height_in, depth_in)
    places = (density, pack_m, width_m, halo_m, height_m, depth_m)
    fetches = [
        pltpu.make_async_copy(src, dst, fetch_sem.at[i]) for i, (src, dst) in enumerate(zip(sources, places))
    ]
    for fetch in fetches:
        fetch.start()

    def remote(src, dst, send, recv_sem, peer):
        return pltpu.make_async_remote_copy(
            src_ref=src, dst_ref=dst, send_sem=send, recv_sem=recv_sem,
            device_id=peer, device_id_type=pl.DeviceIdType.MESH,
        )

    to_left = remote(packed, from_right, tile_send.at[0], tile_recv.at[1], {"tile": t - 1})
    to_right = remote(packed, from_left, tile_send.at[1], tile_recv.at[0], {"tile": t + 1})

    pl.semaphore_wait(
        barrier,
        (d > 0).astype(jnp.int32) + (d < slabs - 1).astype(jnp.int32)
        + (t > 0).astype(jnp.int32) + (t < tiles - 1).astype(jnp.int32),
    )

    def pass_on(r):
        @pl.when((d > 0) & (d + r - 1 < slabs))
        def _():
            signal(ready.at[HIGH, r], {"depth": d - 1})

        @pl.when((d < slabs - 1) & (d - r + 1 >= 0))
        def _():
            signal(ready.at[LOW, r], {"depth": d + 1})

    def hear(r):
        @pl.when(d + r < slabs)
        def _():
            pl.semaphore_wait(ready.at[HIGH, r], 1)

        @pl.when(d - r >= 0)
        def _():
            pl.semaphore_wait(ready.at[LOW, r], 1)

    pass_on(2)

    cuts = [cells * c // CUTS_OF for c in CUTS] + [cells]
    parts = [slice(a, b) for a, b in zip(cuts, cuts[1:])]
    to_below = [
        remote(density_in.at[p], from_side.at[HIGH, p], depth_send.at[0, i], depth_recv.at[1, i], {"depth": d - 1})
        for i, p in enumerate(parts)
    ]
    to_above = [
        remote(density_in.at[p], from_side.at[LOW, p], depth_send.at[1, i], depth_recv.at[0, i], {"depth": d + 1})
        for i, p in enumerate(parts)
    ]

    @pl.when(d > 0)
    def _():
        to_below[0].start()

    @pl.when(d < slabs - 1)
    def _():
        to_above[0].start()

    fetches[0].wait()
    fetches[1].wait()
    whole = jnp.concatenate([density[z] for z in range(cells)], axis=1)
    packed[...] = matmul(whole, pack_m[...]).astype(bf16)

    @pl.when(t > 0)
    def _():
        to_left.start()

    @pl.when(t < tiles - 1)
    def _():
        to_right.start()

    @pl.when(t == 0)
    def _():
        from_left[...] = jnp.zeros_like(from_left)

    @pl.when(t == tiles - 1)
    def _():
        from_right[...] = jnp.zeros_like(from_right)

    @pl.when(d == 0)
    def _():
        from_side[LOW] = jnp.zeros((cells, rows, width), bf16)
        edges_side[LOW] = jnp.zeros((rows, width), bf16)

    @pl.when(d == slabs - 1)
    def _():
        from_side[HIGH] = jnp.zeros((cells, rows, width), bf16)
        edges_side[HIGH] = jnp.zeros((rows, width), bf16)

    pixel = lax.broadcasted_iota(jnp.int32, (rows, rows), 0).astype(jnp.float32)
    cell = lax.broadcasted_iota(jnp.int32, (rows, rows), 1).astype(jnp.float32)
    for v in range(views):
        where_at = zoom[v] * pixel + shift[v]
        table[v * rows : (v + 1) * rows] = jnp.maximum(0.0, 1.0 - jnp.abs(where_at - cell)).astype(bf16)

    def resample(plane, into, v, part):
        at = slice(v * rows, (v + 1) * rows)
        for z in range(part.start, part.stop, 2):
            pair = matmul(table[at], jnp.concatenate([plane(z), plane(z + 1)], axis=1))
            into[z, at] = pair[:, :width]
            into[z + 1, at] = pair[:, width:]

    everything = slice(0, cells)
    for v in range(views):
        resample(lambda z: density[z], sampled, v, everything)
    def blur_plane(block, sides, out, part):
        count = part.stop - part.start
        inside = matmul(block.reshape(count * rows, width), width_m[...])
        outside = matmul(sides, halo_m[:, part.start * width : part.stop * width])
        along_width = jnp.concatenate(
            [inside[z * rows : (z + 1) * rows] + outside[:, z * width : (z + 1) * width] for z in range(count)],
            axis=1,
        ).astype(bf16)
        flat = matmul(height_m[...], along_width).astype(bf16)
        for z in range(count):
            planes[out, part.start + z] = flat[:, z * width : (z + 1) * width]

    chunk = min(CHUNK, group_rows)
    per_group = group_rows // chunk
    extinction = -(EXTINCTION / (cells * slabs)) * LOG2E
    peak = basis - 1

    def coefficients(v, c):
        scale = extinction if c == colours else 1.0
        return [weights[v, c, k] * (math.exp(-0.5 * k * k) * scale) for k in range(basis)]

    def bumps(s, coefs):
        fall = jnp.exp2((-0.5 * peak * peak * LOG2E) * (s * s))
        ratio = jnp.exp2((peak * LOG2E) * s)
        sums = []
        for coef in coefs:
            total = coef[basis - 1] * ratio + coef[basis - 2]
            for k in range(basis - 3, -1, -1):
                total = total * ratio + coef[k]
            sums.append(total)
        return fall, sums

    tap = lax.broadcasted_iota(jnp.int32, (chunk, basis * chunk), 1)
    same = (tap % chunk == lax.broadcasted_iota(jnp.int32, (chunk, basis * chunk), 0)).astype(jnp.float32)
    for v in range(views):
        for c in range(channels):
            coef = coefficients(v, c)
            spread = jnp.zeros((chunk, basis * chunk), jnp.float32)
            for k in range(basis):
                spread = jnp.where(tap // chunk == k, coef[k], spread)
            spread = spread * same
            high = spread.astype(bf16)
            mixing[v, c * chunk : (c + 1) * chunk] = high
            mixing[v, (channels + c) * chunk : (channels + c + 1) * chunk] = (spread - high.astype(jnp.float32)).astype(bf16)

    def terms(s):
        ratio = jnp.exp2((peak * LOG2E) * s)
        each = [jnp.exp2((-0.5 * peak * peak * LOG2E) * (s * s))]
        for _ in range(1, basis):
            each.append(each[-1] * ratio)
        return jnp.concatenate([x.astype(bf16) for x in each], axis=0)

    def light(source, v, part, into, first, passing):
        for z in range(part.start, part.stop, 2):
            pair = [terms(source[y, pl.ds(v * rows + first, chunk), :]) for y in (z, z + 1)]
            mixed = matmul(mixing[v], jnp.concatenate(pair, axis=1))
            mixed = mixed[: channels * chunk] + mixed[channels * chunk :]
            for y in range(2):
                value = [
                    mixed[c * chunk : (c + 1) * chunk, y * width : (y + 1) * width] for c in range(channels)
                ]
                later = passing * jnp.exp2(value[colours])
                share = passing - later
                for c in range(colours):
                    into[v, c, z + y, pl.ds(first, chunk), :] = share * value[c]
                passing = later
        return passing

    def store_alpha(slab_index, v, i, value):
        group = i // per_group
        inside = pl.multiple_of((i % per_group) * chunk, chunk)
        alpha[slab_index, group, v, pl.ds(inside, chunk), :] = value.astype(bf16)

    def transfer(i, carry):
        first = pl.multiple_of(i * chunk, chunk)
        for v in range(views):
            passing = light(sampled, v, everything, lit, first, jnp.ones((chunk, width), jnp.float32))
            store_alpha(d, v, i, 1.0 - passing)
        return carry

    def send_part(i):
        @pl.when(d > 0)
        def _():
            to_below[i].start()

        @pl.when(d < slabs - 1)
        def _():
            to_above[i].start()

    middle = rows // chunk // 2
    lax.fori_loop(0, middle, transfer, 0, unroll=4)
    send_part(1)
    lax.fori_loop(middle, rows // chunk, transfer, 0, unroll=4)

    for fetch in fetches[2:]:
        fetch.wait()

    @pl.when(t > 0)
    def _():
        to_left.wait_send()
        to_right.wait_recv()

    @pl.when(t < tiles - 1)
    def _():
        to_right.wait_send()
        to_left.wait_recv()

    lane = lax.broadcasted_iota(jnp.int32, (rows, width), 1)
    edges[...] = jnp.where(
        lane < cells * RADIUS, from_right[...].astype(jnp.float32), from_left[...].astype(jnp.float32)
    ).astype(bf16)

    edges_below = remote(edges, edges_side.at[HIGH], edge_send.at[0], edge_recv.at[1], {"depth": d - 1})
    edges_above = remote(edges, edges_side.at[LOW], edge_send.at[1], edge_recv.at[0], {"depth": d + 1})

    @pl.when(d > 0)
    def _():
        edges_below.start()

    @pl.when(d < slabs - 1)
    def _():
        edges_above.start()

    send_part(2)
    blur_plane(density[...], edges[...], 1, everything)

    for r in range(2, slabs - 1):
        hear(r)
        if r < slabs - 2:
            pass_on(r + 1)

    def to_renderer(j):
        return remote(alpha.at[d], alpha.at[d], alpha_send.at[j], alpha_recv.at[d], {"depth": j})

    def beside_pair(s, j):
        pair = pl.ds(jnp.where(s == 0, 0, slabs - 2), 2)
        return remote(alpha.at[s, pair], alpha.at[s, pair], alpha_send.at[0], alpha_recv.at[s], {"depth": j})

    next_in = jnp.where(d == 0, 1, slabs - 2)

    def needs(j):
        return (j - d >= 2) | (d - j >= 2)

    outer_first = jnp.where(d == 1, 2 * group_rows, 0)

    def take_outer(part):
        for v in range(views):
            resample(lambda z: from_side[outer_side, z], sampled_outer, v, part)

        def transfer(i, carry):
            first = pl.multiple_of(outer_first + i * chunk, chunk)
            at = pl.ds(first, chunk)
            for v in range(views):
                passing = jnp.ones((chunk, width), jnp.float32) if part.start == 0 else passing_outer[v, at, :]
                passing = light(sampled_outer, v, part, lit_outer, first, passing)
                if part.stop < cells:
                    passing_outer[v, at, :] = passing
                else:
                    store_alpha(outer, v, outer_first // chunk + i, 1.0 - passing)
            return carry

        lax.fori_loop(0, (slabs - 2) * per_group, transfer, 0, unroll=4)

    def take_inner(side, which, part):
        for v in range(views):
            resample(lambda z: from_side[side, z], sampled_inner, v, part)
        for v in range(views):
            coefs = [coefficients(v, colours)]

            def transfer(i, carry, v=v, coefs=coefs):
                at = pl.ds(pl.multiple_of(i * chunk, chunk), chunk)
                power = jnp.zeros((chunk, width), jnp.float32) if part.start == 0 else power_inner[v, at, :]
                for z in range(part.start, part.stop):
                    fall, sums = bumps(
                        sampled_inner[z, pl.ds(pl.multiple_of(v * rows + i * chunk, chunk), chunk), :], coefs
                    )
                    power = power + fall * sums[0]
                if part.stop < cells:
                    power_inner[v, at, :] = power
                else:
                    store_alpha(which, v, i, 1.0 - jnp.exp2(power))
                return carry

            lax.fori_loop(0, rows // chunk, transfer, 0, unroll=2)

    for i, part in enumerate(parts):
        @pl.when(d > 0)
        def _():
            to_below[i].wait_send()
            to_above[i].wait_recv()
            if i == 1:
                edges_below.wait_send()
                edges_above.wait_recv()

        @pl.when(d < slabs - 1)
        def _():
            to_above[i].wait_send()
            to_below[i].wait_recv()
            if i == 1:
                edges_above.wait_send()
                edges_below.wait_recv()

        if i == 1:
            send_part(3)
        if i == 2:
            for j in range(1, slabs - 1):
                @pl.when(needs(j))
                def _():
                    to_renderer(j).start()

            @pl.when(at_end)
            def _():
                beside_pair(d, next_in).start()

        if i:
            ready_part = slice(0, part.stop) if i == 1 else part
            blur_plane(from_side[LOW, ready_part], edges_side[LOW], 0, ready_part)
            blur_plane(from_side[HIGH, ready_part], edges_side[HIGH], 2, ready_part)

        @pl.when(has_outer)
        def _():
            take_outer(part)
            take_inner(inner_side, inner, part)

    if slabs > 4:
        @pl.when(between)
        def _():
            take_inner(LOW, d - 1, everything)
            take_inner(HIGH, d + 1, everything)

    gain = -OCCLUSION_GAIN * LOG2E / tap_total**3

    def occlusion(which, into):
        for g in range(0, rows, 2 * GROUP):
            def column(at):
                part = pl.ds(at, GROUP)
                return planes[:, :, part, :].reshape(3 * cells * GROUP, width)

            both = matmul(depth_m[which], jnp.concatenate([column(g), column(g + GROUP)], axis=1))
            both = jnp.exp2(gain * both).astype(bf16)
            into[:, g : g + GROUP, :] = both[:, :width].reshape(cells, GROUP, width)
            into[:, g + GROUP : g + 2 * GROUP, :] = both[:, width:].reshape(cells, GROUP, width)

    occlusion(1, shade)

    @pl.when(has_outer)
    def _():
        occlusion(2 * outer_side, shade_outer)

    for j in range(1, slabs - 1):
        @pl.when(needs(j))
        def _():
            to_renderer(j).wait_send()

    @pl.when(at_end)
    def _():
        beside_pair(d, next_in).wait_send()

    @pl.when(has_outer)
    def _():
        beside_pair(outer, outer).wait_recv()

    for s in range(slabs):
        far = (s - d >= 2) | (d - s >= 2)

        @pl.when(renders & far)
        def _():
            remote(alpha.at[s], alpha.at[s], alpha_send.at[0], alpha_recv.at[s], {"depth": s}).wait_recv()

    def peer_of(k):
        return lax.rem(d + step * k, slabs)

    def slab_copy(v, k):
        return remote(
            slab.at[v, k], recv[v].at[d], slab_send.at[v, k], slab_recv.at[v, d], {"depth": peer_of(k)}
        )

    def slab_wait(v, s):
        remote(slab.at[v, 0], recv[v].at[s], slab_send.at[v, 0], slab_recv.at[v, s], {"depth": s}).wait_recv()

    def extra_copy(v):
        return remote(extra.at[v], recv_extra.at[v], extra_send.at[v], extra_recv.at[v], {"depth": outer})

    def ahead(v, group, inside):
        passing = jnp.ones((chunk, width), jnp.float32)
        mine = jnp.zeros((chunk, width), jnp.float32)
        beside = jnp.zeros((chunk, width), jnp.float32)
        for q in range(slabs):
            slot = order[v, q]
            dense = alpha[slot, group, v, inside, :].astype(jnp.float32)
            mine = mine + (slot == d).astype(jnp.float32) * passing
            beside = beside + (slot == outer).astype(jnp.float32) * passing
            passing = passing * (1.0 - dense)
        return mine, beside, passing

    def gather(source, shaded, v, at):
        total = [jnp.zeros((chunk, width), jnp.float32)] * colours
        for z in range(cells):
            s = shaded[z, pl.ds(v * rows + at, chunk), :]
            total = [total[c] + source[v, c, z, pl.ds(at, chunk), :] * s for c in range(colours)]
        return total

    spans = [slice(i * chunk, (i + 1) * chunk) for i in range(per_group)]

    @pl.when(has_outer)
    def _():
        for v in range(views):
            for inside in spans:
                _, beside, passing = ahead(v, outer, inside)
                extra[v, 0, inside, :] = beside.astype(bf16)
                extra[v, 1, inside, :] = (1.0 - passing).astype(bf16)
            extra_copy(v).start()

    steps = sorted(range(1, slabs - 1), key=lambda k: abs(2 * k - slabs)) + [slabs - 1]
    for v in range(views):
        resample(lambda z: shade[z], sampled, v, everything)

        @pl.when(has_outer)
        def _():
            resample(lambda z: shade_outer[z], sampled_outer, v, everything)

        for k in steps + [0]:
            group = peer_of(k)
            start = pl.multiple_of(group * group_rows, group_rows)
            if k == 0:
                for inside in spans:
                    total = gather(lit, sampled, v, start + inside.start)
                    for c in range(colours):
                        own[v, c, inside, :] = total[c]
                continue

            def fill(with_outer):
                for inside in spans:
                    at = start + inside.start
                    mine, beside, _ = ahead(v, group, inside)
                    total = [mine * x for x in gather(lit, sampled, v, at)]
                    if with_outer and k < slabs - 1:
                        other = gather(lit_outer, sampled_outer, v, at)
                        total = [total[c] + beside * other[c] for c in range(colours)]
                    for c in range(colours):
                        slab[v, k, c, inside, :] = total[c].astype(bf16)

            @pl.when(has_outer)
            def _():
                fill(True)
                slab_copy(v, k).start()

            if slabs > 4:
                @pl.when(between)
                def _():
                    fill(False)
                    slab_copy(v, k).start()

            if k == 1:
                @pl.when(at_end)
                def _():
                    for inside in spans:
                        total = gather(lit, sampled, v, start + inside.start)
                        for c in range(colours):
                            slab[v, k, c, inside, :] = total[c].astype(bf16)
                    slab_copy(v, k).start()

    for v in range(views):
        @pl.when(at_end)
        def _():
            remote(
                extra.at[v], recv_extra.at[v], extra_send.at[v], extra_recv.at[v], {"depth": outer}
            ).wait_recv()
            for c in range(colours):
                image[v, c] = recv_extra[v, 0].astype(jnp.float32) * own[v, c]
            image[v, colours] = recv_extra[v, 1].astype(jnp.float32)

        if slabs > 4:
            @pl.when(between)
            def _():
                for inside in spans:
                    mine, _, passing = ahead(v, d, inside)
                    for c in range(colours):
                        image[v, c, inside, :] = mine * own[v, c, inside, :]
                    image[v, colours, inside, :] = 1.0 - passing

        @pl.when(has_outer)
        def _():
            slab_wait(v, outer)
            for inside in spans:
                mine, beside, passing = ahead(v, d, inside)
                for c in range(colours):
                    image[v, c, inside, :] = (
                        mine * own[v, c, inside, :] + beside * recv[v][outer, c, inside, :].astype(jnp.float32)
                    )
                image[v, colours, inside, :] = 1.0 - passing

    for v in range(views):
        for s in range(1, slabs - 1):
            @pl.when(d != s)
            def _():
                slab_wait(v, s)
                for c in range(colours):
                    image[v, c] = image[v, c] + recv[v][s, c].astype(jnp.float32)

    for v in range(views):
        for k in range(1, slabs):
            sends = renders | at_end if k == 1 else renders

            @pl.when(sends)
            def _():
                slab_copy(v, k).wait_send()

        @pl.when(has_outer)
        def _():
            extra_copy(v).wait_send()


def local(slabs, tiles, density, view_zoom, view_shift, tf_weights, perm_order):
    cells, rows, width = density.shape
    views, channels, basis = tf_weights.shape
    group_rows = rows // slabs
    chunk = min(CHUNK, group_rows)
    matrices, tap_total = constants(cells, rows, width)
    hbm = pl.BlockSpec(memory_space=pltpu.HBM)
    smem = pl.BlockSpec(memory_space=pltpu.SMEM)
    bf16, f32 = jnp.bfloat16, jnp.float32
    block = pltpu.VMEM((cells, rows, width), bf16)
    edge = pltpu.VMEM((rows, width), bf16)
    samples = pltpu.VMEM((cells, views * rows, width), f32)
    emitted = pltpu.VMEM((views, channels - 1, cells, rows, width), f32)
    per_pixel = pltpu.VMEM((views, rows, width), f32)
    dma = pltpu.SemaphoreType.DMA
    operands = (density, view_zoom, view_shift, tf_weights, perm_order, *matrices)
    return pl.pallas_call(
        functools.partial(kernel, slabs, tiles, tap_total),
        out_shape=pltpu.VMEM((views, channels, group_rows, width), f32),
        in_specs=[hbm, smem, smem, smem, smem] + [hbm] * len(matrices),
        out_specs=pl.BlockSpec(memory_space=pltpu.VMEM),
        scratch_shapes=[block]
        + [pltpu.VMEM(m.shape, bf16) for m in matrices]
        + [
            pltpu.VMEM((views * rows, rows), bf16),
            edge, edge, edge, edge, pltpu.VMEM((2, rows, width), bf16),
            pltpu.VMEM((3, cells, rows, width), bf16), pltpu.VMEM((2, cells, rows, width), bf16),
            samples, samples, samples, emitted, emitted, block, block,
            pltpu.VMEM((views, 2 * channels * chunk, basis * chunk), bf16),
            per_pixel, per_pixel,
            pltpu.VMEM((slabs, slabs, views, group_rows, width), bf16),
            pltpu.VMEM((views, slabs, channels - 1, group_rows, width), bf16),
            pltpu.VMEM((views, channels - 1, group_rows, width), f32),
            pltpu.VMEM((views, 2, group_rows, width), bf16),
            pltpu.VMEM((views, 2, group_rows, width), bf16),
        ]
        + [pltpu.VMEM((slabs, channels - 1, group_rows, width), bf16)] * views
        + [dma((1 + len(matrices),)), dma((2,)), dma((2,)), dma((2, len(CUTS))), dma((2, len(CUTS))), dma((2,)), dma((2,))]
        + [dma((slabs,)), dma((slabs,))]
        + [dma((views, slabs)), dma((views, slabs)), dma((views,)), dma((views,))]
        + [pltpu.SemaphoreType.REGULAR((2, slabs))],
        compiler_params=pltpu.CompilerParams(
            collective_id=0, has_side_effects=True, vmem_limit_bytes=48 * 1024 * 1024
        ),
    )(*[pltpu.with_memory_space_constraint(x, pltpu.HBM) for x in operands])


def solution(mesh):
    placed = (P("depth", None, "tile"), P(), P(), P(), P())
    return jax.shard_map(
        functools.partial(local, mesh.shape["depth"], mesh.shape["tile"]),
        mesh=mesh, in_specs=placed, out_specs=P(None, None, "depth", "tile"), check_vma=False,
    )
```

```python
import functools
import math

import jax
import jax.numpy as jnp
import numpy as np
from jax import lax
from jax.experimental import pallas as pl
from jax.experimental.pallas import tpu as pltpu
from jax.sharding import PartitionSpec as P

RADIUS = 8
OCCLUSION_GAIN = 1.5
EXTINCTION = 0.5
LOG2E = math.log2(math.e)
GROUP = 16
CHUNK = 32
CUTS = (0, 2, 4, 6)
CUTS_OF = 8
ALPHA_AT = 2


def rounded_taps():
    offsets = np.arange(-RADIUS, RADIUS + 1, dtype=np.float64)
    taps = np.exp(-offsets * offsets / 72.0)
    taps = (taps / taps.sum()).astype(jnp.bfloat16).astype(np.float64)
    return taps, float(taps.sum())


def band(out_count, in_count, shift, taps):
    offset = np.arange(in_count)[None, :] + shift - np.arange(out_count)[:, None]
    inside = np.abs(offset) <= RADIUS
    return np.where(inside, taps[np.clip(offset + RADIUS, 0, 2 * RADIUS)], 0.0)


def constants(cells, rows, width):
    taps, total = rounded_taps()
    pack = np.zeros((cells, width, width), np.float32)
    low = np.zeros((width, cells, width))
    high = np.zeros((width, cells, width))
    half = cells * RADIUS
    from_low = band(width, RADIUS, -RADIUS, taps).T
    from_high = band(width, RADIUS, width, taps).T
    for z in range(cells):
        for j in range(RADIUS):
            pack[z, j, z * RADIUS + j] = 1.0
            pack[z, width - RADIUS + j, half + z * RADIUS + j] = 1.0
        low[half + z * RADIUS : half + (z + 1) * RADIUS, z] = from_low
        high[z * RADIUS : (z + 1) * RADIUS, z] = from_high
    halo = (low + high).reshape(width, cells * width)
    depth = np.stack([np.kron(band(cells, 3 * cells, -s * cells, taps), np.eye(GROUP)) for s in (0, 1, 2)])
    arrays = (
        pack.reshape(cells * width, width),
        band(width, width, 0, taps).T,
        halo,
        band(rows, rows, 0, taps),
        depth,
    )
    return [jnp.asarray(a.astype(jnp.bfloat16)) for a in arrays], total


def matmul(a, b):
    return jnp.dot(a, b, preferred_element_type=jnp.float32)


def kernel(
    slabs, tiles, tap_total,
    density_in, zoom_in, shift_in, weights_in, order_in, pack_in, width_in, halo_in, height_in, depth_in,
    image,
    zoom, shift, weights, order, density, pack_m, width_m, halo_m, height_m, depth_m,
    table, packed, from_left, from_right, edges, edges_side,
    planes, from_side, sampled, sampled_outer, sampled_inner, lit, lit_outer, shade, shade_outer,
    mixing, passing_outer, power_inner, alpha, slab, own, *rest,
):
    views, channels, basis = weights_in.shape
    cells, rows, width = density_in.shape
    recv = rest[:views]
    (
        small_sem, fetch_sem, tile_send, tile_recv, depth_send, depth_recv, edge_send, edge_recv,
        alpha_send, alpha_recv, slab_send, slab_recv, end_send, end_recv, ready,
    ) = rest[views:]
    group_rows = rows // slabs
    d = lax.axis_index("depth")
    t = lax.axis_index("tile")
    bf16 = jnp.bfloat16
    LOW, HIGH = 0, 1
    colours = channels - 1

    renders = (d > 0) & (d < slabs - 1)
    has_outer = (d == 1) | (d == slabs - 2)
    between = (d > 1) & (d < slabs - 2)
    at_end = (d == 0) | (d == slabs - 1)
    outer_side = jnp.where(d == 1, LOW, HIGH)
    outer = jnp.where(d == 1, 0, slabs - 1)
    inner_side = 1 - outer_side
    inner = jnp.where(d == 1, 2, d - 1)
    step = jnp.where(2 * d < slabs, 1, slabs - 1)

    barrier = pltpu.get_barrier_semaphore()

    def signal(sem, peer):
        pl.semaphore_signal(sem, inc=1, device_id=peer, device_id_type=pl.DeviceIdType.MESH)

    @pl.when(d > 0)
    def _():
        signal(barrier, {"depth": d - 1})

    @pl.when(d < slabs - 1)
    def _():
        signal(barrier, {"depth": d + 1})

    @pl.when(t > 0)
    def _():
        signal(barrier, {"tile": t - 1})

    @pl.when(t < tiles - 1)
    def _():
        signal(barrier, {"tile": t + 1})

    sources = (density_in, pack_in, width_in, halo_in, height_in, depth_in)
    places = (density, pack_m, width_m, halo_m, height_m, depth_m)
    fetches = [
        pltpu.make_async_copy(src, dst, fetch_sem.at[i]) for i, (src, dst) in enumerate(zip(sources, places))
    ]
    smalls = [
        pltpu.make_async_copy(src, dst, small_sem.at[i])
        for i, (src, dst) in enumerate(zip((zoom_in, shift_in, weights_in, order_in), (zoom, shift, weights, order)))
    ]
    for fetch in smalls + fetches:
        fetch.start()

    def remote(src, dst, send, recv_sem, peer):
        return pltpu.make_async_remote_copy(
            src_ref=src, dst_ref=dst, send_sem=send, recv_sem=recv_sem,
            device_id=peer, device_id_type=pl.DeviceIdType.MESH,
        )

    to_left = remote(packed, from_right, tile_send.at[0], tile_recv.at[1], {"tile": t - 1})
    to_right = remote(packed, from_left, tile_send.at[1], tile_recv.at[0], {"tile": t + 1})

    pl.semaphore_wait(
        barrier,
        (d > 0).astype(jnp.int32) + (d < slabs - 1).astype(jnp.int32)
        + (t > 0).astype(jnp.int32) + (t < tiles - 1).astype(jnp.int32),
    )

    def pass_on(r):
        @pl.when((d > 0) & (d + r - 1 < slabs))
        def _():
            signal(ready.at[HIGH, r], {"depth": d - 1})

        @pl.when((d < slabs - 1) & (d - r + 1 >= 0))
        def _():
            signal(ready.at[LOW, r], {"depth": d + 1})

    def hear(r):
        @pl.when(d + r < slabs)
        def _():
            pl.semaphore_wait(ready.at[HIGH, r], 1)

        @pl.when(d - r >= 0)
        def _():
            pl.semaphore_wait(ready.at[LOW, r], 1)

    pass_on(2)

    cuts = [cells * c // CUTS_OF for c in CUTS] + [cells]
    parts = [slice(a, b) for a, b in zip(cuts, cuts[1:])]
    to_below = [
        remote(density_in.at[p], from_side.at[HIGH, p], depth_send.at[0, i], depth_recv.at[1, i], {"depth": d - 1})
        for i, p in enumerate(parts)
    ]
    to_above = [
        remote(density_in.at[p], from_side.at[LOW, p], depth_send.at[1, i], depth_recv.at[0, i], {"depth": d + 1})
        for i, p in enumerate(parts)
    ]

    @pl.when(d > 0)
    def _():
        to_below[0].start()

    @pl.when(d < slabs - 1)
    def _():
        to_above[0].start()

    fetches[0].wait()
    fetches[1].wait()
    whole = jnp.concatenate([density[z] for z in range(cells)], axis=1)
    packed[...] = matmul(whole, pack_m[...]).astype(bf16)

    @pl.when(t > 0)
    def _():
        to_left.start()

    @pl.when(t < tiles - 1)
    def _():
        to_right.start()

    @pl.when(t == 0)
    def _():
        from_left[...] = jnp.zeros_like(from_left)

    @pl.when(t == tiles - 1)
    def _():
        from_right[...] = jnp.zeros_like(from_right)

    @pl.when(d == 0)
    def _():
        from_side[LOW] = jnp.zeros((cells, rows, width), bf16)
        edges_side[LOW] = jnp.zeros((rows, width), bf16)

    @pl.when(d == slabs - 1)
    def _():
        from_side[HIGH] = jnp.zeros((cells, rows, width), bf16)
        edges_side[HIGH] = jnp.zeros((rows, width), bf16)

    for fetch in smalls:
        fetch.wait()

    pixel = lax.broadcasted_iota(jnp.int32, (rows, rows), 0).astype(jnp.float32)
    cell = lax.broadcasted_iota(jnp.int32, (rows, rows), 1).astype(jnp.float32)
    for v in range(views):
        where_at = zoom[v] * pixel + shift[v]
        table[v * rows : (v + 1) * rows] = jnp.maximum(0.0, 1.0 - jnp.abs(where_at - cell)).astype(bf16)

    def resample(plane, into, v, part):
        at = slice(0, views * rows) if v is None else slice(v * rows, (v + 1) * rows)
        for z in range(part.start, part.stop, 2):
            pair = matmul(table[at], jnp.concatenate([plane(z), plane(z + 1)], axis=1))
            into[z, at] = pair[:, :width]
            into[z + 1, at] = pair[:, width:]

    everything = slice(0, cells)
    resample(lambda z: density[z], sampled, None, everything)
    def blur_plane(block, sides, out, part):
        count = part.stop - part.start
        inside = matmul(block.reshape(count * rows, width), width_m[...])
        outside = matmul(sides, halo_m[:, part.start * width : part.stop * width])
        along_width = jnp.concatenate(
            [inside[z * rows : (z + 1) * rows] + outside[:, z * width : (z + 1) * width] for z in range(count)],
            axis=1,
        ).astype(bf16)
        flat = matmul(height_m[...], along_width).astype(bf16)
        for z in range(count):
            planes[out, part.start + z] = flat[:, z * width : (z + 1) * width]

    chunk = min(CHUNK, group_rows)
    per_group = group_rows // chunk
    extinction = -(EXTINCTION / (cells * slabs)) * LOG2E
    peak = basis - 1

    def coefficients(v, c):
        scale = extinction if c == colours else 1.0
        return [weights[v, c, k] * (math.exp(-0.5 * k * k) * scale) for k in range(basis)]

    def bumps(s, coefs):
        fall = jnp.exp2((-0.5 * peak * peak * LOG2E) * (s * s))
        ratio = jnp.exp2((peak * LOG2E) * s)
        sums = []
        for coef in coefs:
            total = coef[basis - 1] * ratio + coef[basis - 2]
            for k in range(basis - 3, -1, -1):
                total = total * ratio + coef[k]
            sums.append(total)
        return fall, sums

    tap = lax.broadcasted_iota(jnp.int32, (chunk, basis * chunk), 1)
    same = (tap % chunk == lax.broadcasted_iota(jnp.int32, (chunk, basis * chunk), 0)).astype(jnp.float32)
    for v in range(views):
        for c in range(channels):
            coef = coefficients(v, c)
            spread = jnp.zeros((chunk, basis * chunk), jnp.float32)
            for k in range(basis):
                spread = jnp.where(tap // chunk == k, coef[k], spread)
            spread = spread * same
            high = spread.astype(bf16)
            mixing[v, c * chunk : (c + 1) * chunk] = high
            mixing[v, (channels + c) * chunk : (channels + c + 1) * chunk] = (spread - high.astype(jnp.float32)).astype(bf16)

    def terms(s):
        ratio = jnp.exp2((peak * LOG2E) * s)
        each = [jnp.exp2((-0.5 * peak * peak * LOG2E) * (s * s))]
        for _ in range(1, basis):
            each.append(each[-1] * ratio)
        return jnp.concatenate([x.astype(bf16) for x in each], axis=0)

    def light(source, v, part, into, first, passing):
        for z in range(part.start, part.stop, 2):
            pair = [terms(source[y, pl.ds(v * rows + first, chunk), :]) for y in (z, z + 1)]
            mixed = matmul(mixing[v], jnp.concatenate(pair, axis=1))
            mixed = mixed[: channels * chunk] + mixed[channels * chunk :]
            for y in range(2):
                value = [
                    mixed[c * chunk : (c + 1) * chunk, y * width : (y + 1) * width] for c in range(channels)
                ]
                later = passing * jnp.exp2(value[colours])
                share = passing - later
                for c in range(colours):
                    into[v, c, z + y, pl.ds(first, chunk), :] = share * value[c]
                passing = later
        return passing

    def store_alpha(slab_index, v, i, value):
        group = i // per_group
        inside = pl.multiple_of((i % per_group) * chunk, chunk)
        alpha[slab_index, group, v, pl.ds(inside, chunk), :] = value.astype(bf16)

    def transfer(i, carry):
        first = pl.multiple_of(i * chunk, chunk)
        for v in range(views):
            passing = light(sampled, v, everything, lit, first, jnp.ones((chunk, width), jnp.float32))
            store_alpha(d, v, i, 1.0 - passing)
        return carry

    def send_part(i):
        @pl.when(d > 0)
        def _():
            to_below[i].start()

        @pl.when(d < slabs - 1)
        def _():
            to_above[i].start()

    middle = rows // chunk // 2
    lax.fori_loop(0, middle, transfer, 0, unroll=4)
    send_part(1)
    lax.fori_loop(middle, rows // chunk, transfer, 0, unroll=4)

    for fetch in fetches[2:]:
        fetch.wait()

    @pl.when(t > 0)
    def _():
        to_left.wait_send()
        to_right.wait_recv()

    @pl.when(t < tiles - 1)
    def _():
        to_right.wait_send()
        to_left.wait_recv()

    lane = lax.broadcasted_iota(jnp.int32, (rows, width), 1)
    edges[...] = jnp.where(
        lane < cells * RADIUS, from_right[...].astype(jnp.float32), from_left[...].astype(jnp.float32)
    ).astype(bf16)

    edges_below = remote(edges, edges_side.at[HIGH], edge_send.at[0], edge_recv.at[1], {"depth": d - 1})
    edges_above = remote(edges, edges_side.at[LOW], edge_send.at[1], edge_recv.at[0], {"depth": d + 1})

    @pl.when(d > 0)
    def _():
        edges_below.start()

    @pl.when(d < slabs - 1)
    def _():
        edges_above.start()

    send_part(2)
    blur_plane(density[...], edges[...], 1, everything)

    for r in range(2, slabs):
        hear(r)
        if r < slabs - 1:
            pass_on(r + 1)

    def to_renderer(j):
        return remote(alpha.at[d], alpha.at[d], alpha_send.at[j], alpha_recv.at[d], {"depth": j})

    def beside_pair(s, j):
        pair = pl.ds(jnp.where(s == 0, 0, slabs - 2), 2)
        return remote(alpha.at[s, pair], alpha.at[s, pair], alpha_send.at[0], alpha_recv.at[s], {"depth": j})

    def to_end(i, s):
        g = i * (slabs - 1)
        return remote(alpha.at[s, g], alpha.at[s, g], end_send.at[i], end_recv.at[s], {"depth": g})

    next_in = jnp.where(d == 0, 1, slabs - 2)

    def needs(j):
        return (j - d >= 2) | (d - j >= 2)

    outer_first = jnp.where(d == 1, 2 * group_rows, 0)

    def outer_chunk(part, i):
        first = pl.multiple_of(outer_first + i * chunk, chunk)
        at = pl.ds(first, chunk)
        for v in range(views):
            passing = jnp.ones((chunk, width), jnp.float32) if part.start == 0 else passing_outer[v, at, :]
            passing = light(sampled_outer, v, part, lit_outer, first, passing)
            if part.stop < cells:
                passing_outer[v, at, :] = passing
            else:
                store_alpha(outer, v, outer_first // chunk + i, 1.0 - passing)

    def inner_chunk(part, which, i):
        for v in range(views):
            at = slice(i * chunk, (i + 1) * chunk)
            coefs = [coefficients(v, colours)]
            power = jnp.zeros((chunk, width), jnp.float32) if part.start == 0 else power_inner[v, at, :]
            for z in range(part.start, part.stop):
                fall, sums = bumps(sampled_inner[z, v * rows + i * chunk : v * rows + (i + 1) * chunk, :], coefs)
                power = power + fall * sums[0]
            if part.stop < cells:
                power_inner[v, at, :] = power
            else:
                store_alpha(which, v, i, 1.0 - jnp.exp2(power))

    def take_inner(side, which, part):
        resample(lambda z: from_side[side, z], sampled_inner, None, part)
        for i in range(rows // chunk):
            inner_chunk(part, which, i)

    def take_sides(part):
        resample(lambda z: from_side[outer_side, z], sampled_outer, None, part)
        resample(lambda z: from_side[inner_side, z], sampled_inner, None, part)
        count, total = (slabs - 2) * per_group, rows // chunk
        for i in range(count):
            outer_chunk(part, i)
            for j in range(total * i // count, total * (i + 1) // count):
                inner_chunk(part, inner, j)

    for i, part in enumerate(parts):
        @pl.when(d > 0)
        def _():
            to_below[i].wait_send()
            to_above[i].wait_recv()
            if i == 1:
                edges_below.wait_send()
                edges_above.wait_recv()

        @pl.when(d < slabs - 1)
        def _():
            to_above[i].wait_send()
            to_below[i].wait_recv()
            if i == 1:
                edges_above.wait_send()
                edges_below.wait_recv()

        if i == 1:
            send_part(3)
        if i == ALPHA_AT:
            for j in range(1, slabs - 1):
                @pl.when(needs(j))
                def _():
                    to_renderer(j).start()

            @pl.when(at_end)
            def _():
                beside_pair(d, next_in).start()

        if i:
            ready_part = slice(0, part.stop) if i == 1 else part
            blur_plane(from_side[LOW, ready_part], edges_side[LOW], 0, ready_part)
            blur_plane(from_side[HIGH, ready_part], edges_side[HIGH], 2, ready_part)

        @pl.when(has_outer)
        def _():
            take_sides(part)

    if slabs > 4:
        @pl.when(between)
        def _():
            take_inner(LOW, d - 1, everything)
            take_inner(HIGH, d + 1, everything)

    for j in range(2):
        @pl.when(d != j * (slabs - 1))
        def _():
            to_end(j, d).start()

    gain = -OCCLUSION_GAIN * LOG2E / tap_total**3

    def occlusion(matrices, into):
        for g in range(0, rows, 2 * GROUP):
            def column(at):
                part = pl.ds(at, GROUP)
                return planes[:, :, part, :].reshape(3 * cells * GROUP, width)

            both = matmul(matrices, jnp.concatenate([column(g), column(g + GROUP)], axis=1))
            both = jnp.exp2(gain * both).astype(bf16)
            for i, block in enumerate(into):
                mine = both[i * cells * GROUP : (i + 1) * cells * GROUP]
                block[:, g : g + GROUP, :] = mine[:, :width].reshape(cells, GROUP, width)
                block[:, g + GROUP : g + 2 * GROUP, :] = mine[:, width:].reshape(cells, GROUP, width)

    @pl.when(has_outer)
    def _():
        occlusion(jnp.concatenate([depth_m[1], depth_m[2 * outer_side]], axis=0), [shade, shade_outer])

    @pl.when(at_end | between)
    def _():
        occlusion(depth_m[1], [shade])

    resample(lambda z: shade[z], sampled, None, everything)

    @pl.when(has_outer)
    def _():
        resample(lambda z: shade_outer[z], sampled_outer, None, everything)

    @pl.when(has_outer)
    def _():
        beside_pair(outer, outer).wait_recv()

    for s in range(slabs):
        far = (s - d >= 2) | (d - s >= 2)

        @pl.when(renders & far)
        def _():
            remote(alpha.at[s], alpha.at[s], alpha_send.at[0], alpha_recv.at[s], {"depth": s}).wait_recv()

    def peer_of(k):
        return lax.rem(d + step * k, slabs)

    def slab_copy(v, k):
        return remote(
            slab.at[v, k], recv[v].at[d], slab_send.at[v, k], slab_recv.at[v, d], {"depth": peer_of(k)}
        )

    def slab_wait(v, s):
        remote(slab.at[v, 0], recv[v].at[s], slab_send.at[v, 0], slab_recv.at[v, s], {"depth": s}).wait_recv()

    def ahead(v, group, inside):
        passing = jnp.ones((chunk, width), jnp.float32)
        mine = jnp.zeros((chunk, width), jnp.float32)
        beside = jnp.zeros((chunk, width), jnp.float32)
        for q in range(slabs):
            slot = order[v, q]
            dense = alpha[slot, group, v, inside, :].astype(jnp.float32)
            mine = mine + (slot == d).astype(jnp.float32) * passing
            beside = beside + (slot == outer).astype(jnp.float32) * passing
            passing = passing * (1.0 - dense)
        return mine, beside, passing

    def gather(source, shaded, v, at):
        total = [jnp.zeros((chunk, width), jnp.float32)] * colours
        for z in range(cells):
            s = shaded[z, pl.ds(v * rows + at, chunk), :]
            total = [total[c] + source[v, c, z, pl.ds(at, chunk), :] * s for c in range(colours)]
        return total

    spans = [slice(i * chunk, (i + 1) * chunk) for i in range(per_group)]

    steps = sorted(range(1, slabs - 1), key=lambda k: abs(2 * k - slabs)) + [slabs - 1]
    for v in range(views):
        for k in steps + [0]:
            group = peer_of(k)
            start = pl.multiple_of(group * group_rows, group_rows)
            if k == 0:
                for inside in spans:
                    total = gather(lit, sampled, v, start + inside.start)
                    for c in range(colours):
                        own[v, c, inside, :] = total[c]
                continue

            def fill(with_outer):
                for inside in spans:
                    at = start + inside.start
                    mine, beside, _ = ahead(v, group, inside)
                    total = [mine * x for x in gather(lit, sampled, v, at)]
                    if with_outer and k < slabs - 1:
                        other = gather(lit_outer, sampled_outer, v, at)
                        total = [total[c] + beside * other[c] for c in range(colours)]
                    for c in range(colours):
                        slab[v, k, c, inside, :] = total[c].astype(bf16)

            @pl.when(has_outer)
            def _():
                fill(True)
                slab_copy(v, k).start()

            if slabs > 4:
                @pl.when(between)
                def _():
                    fill(False)
                    slab_copy(v, k).start()

            if k == 1:
                @pl.when(at_end)
                def _():
                    for inside in spans:
                        total = gather(lit, sampled, v, start + inside.start)
                        for c in range(colours):
                            slab[v, k, c, inside, :] = total[c].astype(bf16)
                    slab_copy(v, k).start()

    for j in range(1, slabs - 1):
        @pl.when(needs(j))
        def _():
            to_renderer(j).wait_send()

    for j in range(2):
        @pl.when(d != j * (slabs - 1))
        def _():
            to_end(j, d).wait_send()

        @pl.when(d == j * (slabs - 1))
        def _():
            for s in range(slabs):
                if s != j * (slabs - 1):
                    to_end(j, s).wait_recv()

    @pl.when(at_end)
    def _():
        beside_pair(d, next_in).wait_send()

    for v in range(views):
        @pl.when(at_end | between)
        def _():
            for inside in spans:
                mine, _, passing = ahead(v, d, inside)
                for c in range(colours):
                    image[v, c, inside, :] = mine * own[v, c, inside, :]
                image[v, colours, inside, :] = 1.0 - passing

        @pl.when(has_outer)
        def _():
            slab_wait(v, outer)
            for inside in spans:
                mine, beside, passing = ahead(v, d, inside)
                for c in range(colours):
                    image[v, c, inside, :] = (
                        mine * own[v, c, inside, :] + beside * recv[v][outer, c, inside, :].astype(jnp.float32)
                    )
                image[v, colours, inside, :] = 1.0 - passing

    for v in range(views):
        for s in range(1, slabs - 1):
            @pl.when(d != s)
            def _():
                slab_wait(v, s)
                for c in range(colours):
                    image[v, c] = image[v, c] + recv[v][s, c].astype(jnp.float32)

    for v in range(views):
        for k in range(1, slabs):
            sends = renders | at_end if k == 1 else renders

            @pl.when(sends)
            def _():
                slab_copy(v, k).wait_send()


def local(slabs, tiles, density, view_zoom, view_shift, tf_weights, perm_order):
    cells, rows, width = density.shape
    views, channels, basis = tf_weights.shape
    group_rows = rows // slabs
    chunk = min(CHUNK, group_rows)
    matrices, tap_total = constants(cells, rows, width)
    hbm = pl.BlockSpec(memory_space=pltpu.HBM)
    bf16, f32 = jnp.bfloat16, jnp.float32
    block = pltpu.VMEM((cells, rows, width), bf16)
    edge = pltpu.VMEM((rows, width), bf16)
    samples = pltpu.VMEM((cells, views * rows, width), f32)
    emitted = pltpu.VMEM((views, channels - 1, cells, rows, width), f32)
    per_pixel = pltpu.VMEM((views, rows, width), f32)
    dma = pltpu.SemaphoreType.DMA
    operands = (density, view_zoom, view_shift, tf_weights, perm_order, *matrices)
    return pl.pallas_call(
        functools.partial(kernel, slabs, tiles, tap_total),
        out_shape=pltpu.VMEM((views, channels, group_rows, width), f32),
        in_specs=[hbm] * len(operands),
        out_specs=pl.BlockSpec(memory_space=pltpu.VMEM),
        scratch_shapes=[pltpu.SMEM(x.shape, x.dtype) for x in operands[1:5]]
        + [block]
        + [pltpu.VMEM(m.shape, bf16) for m in matrices]
        + [
            pltpu.VMEM((views * rows, rows), bf16),
            edge, edge, edge, edge, pltpu.VMEM((2, rows, width), bf16),
            pltpu.VMEM((3, cells, rows, width), bf16), pltpu.VMEM((2, cells, rows, width), bf16),
            samples, samples, samples, emitted, emitted, block, block,
            pltpu.VMEM((views, 2 * channels * chunk, basis * chunk), bf16),
            per_pixel, per_pixel,
            pltpu.VMEM((slabs, slabs, views, group_rows, width), bf16),
            pltpu.VMEM((views, slabs, channels - 1, group_rows, width), bf16),
            pltpu.VMEM((views, channels - 1, group_rows, width), f32),
        ]
        + [pltpu.VMEM((slabs, channels - 1, group_rows, width), bf16)] * views
        + [dma((4,)), dma((1 + len(matrices),)), dma((2,)), dma((2,)), dma((2, len(CUTS))), dma((2, len(CUTS))), dma((2,)), dma((2,))]
        + [dma((slabs,)), dma((slabs,))]
        + [dma((views, slabs)), dma((views, slabs)), dma((2,)), dma((slabs,))]
        + [pltpu.SemaphoreType.REGULAR((2, slabs))],
        compiler_params=pltpu.CompilerParams(
            collective_id=0, has_side_effects=True, vmem_limit_bytes=48 * 1024 * 1024
        ),
    )(*[pltpu.with_memory_space_constraint(x, pltpu.HBM) for x in operands])


def solution(mesh):
    placed = (P("depth", None, "tile"), P(), P(), P(), P())
    return jax.shard_map(
        functools.partial(local, mesh.shape["depth"], mesh.shape["tile"]),
        mesh=mesh, in_specs=placed, out_specs=P(None, None, "depth", "tile"), check_vma=False,
    )
```

```python
import functools
import math

import jax
import jax.numpy as jnp
import numpy as np
from jax import lax
from jax.experimental import pallas as pl
from jax.experimental.pallas import tpu as pltpu
from jax.sharding import PartitionSpec as P

RADIUS = 8
OCCLUSION_GAIN = 1.5
EXTINCTION = 0.5
LOG2E = math.log2(math.e)
GROUP = 16
CHUNK = 32
CUTS = (0, 2, 4, 6)
CUTS_OF = 8
ALPHA_AT = 2


def rounded_taps():
    offsets = np.arange(-RADIUS, RADIUS + 1, dtype=np.float64)
    taps = np.exp(-offsets * offsets / 72.0)
    taps = (taps / taps.sum()).astype(jnp.bfloat16).astype(np.float64)
    return taps, float(taps.sum())


def band(out_count, in_count, shift, taps):
    offset = np.arange(in_count)[None, :] + shift - np.arange(out_count)[:, None]
    inside = np.abs(offset) <= RADIUS
    return np.where(inside, taps[np.clip(offset + RADIUS, 0, 2 * RADIUS)], 0.0)


def constants(cells, rows, width):
    taps, total = rounded_taps()
    pack = np.zeros((cells, width, width), np.float32)
    low = np.zeros((width, cells, width))
    high = np.zeros((width, cells, width))
    half = cells * RADIUS
    from_low = band(width, RADIUS, -RADIUS, taps).T
    from_high = band(width, RADIUS, width, taps).T
    for z in range(cells):
        for j in range(RADIUS):
            pack[z, j, z * RADIUS + j] = 1.0
            pack[z, width - RADIUS + j, half + z * RADIUS + j] = 1.0
        low[half + z * RADIUS : half + (z + 1) * RADIUS, z] = from_low
        high[z * RADIUS : (z + 1) * RADIUS, z] = from_high
    halo = (low + high).reshape(width, cells * width)
    depth = np.stack([np.kron(band(cells, 3 * cells, -s * cells, taps), np.eye(GROUP)) for s in (0, 1, 2)])
    arrays = (
        pack.reshape(cells * width, width),
        band(width, width, 0, taps).T,
        halo,
        band(rows, rows, 0, taps),
        depth,
    )
    return [jnp.asarray(a.astype(jnp.bfloat16)) for a in arrays], total


def matmul(a, b):
    return jnp.dot(a, b, preferred_element_type=jnp.float32)


def kernel(
    slabs, tiles, tap_total,
    density_in, zoom_in, shift_in, weights_in, order_in, pack_in, width_in, halo_in, height_in, depth_in,
    image,
    zoom, shift, weights, order, density, pack_m, width_m, halo_m, height_m, depth_m,
    table, packed, from_left, from_right, edges, edges_side,
    planes, from_side, sampled, sampled_outer, sampled_inner, lit, lit_outer, shade, shade_outer,
    mixing, passing_outer, power_inner, alpha, slab, own, *rest,
):
    views, channels, basis = weights_in.shape
    cells, rows, width = density_in.shape
    recv = rest[:views]
    (
        small_sem, fetch_sem, tile_send, tile_recv, depth_send, depth_recv, edge_send, edge_recv,
        alpha_send, alpha_recv, slab_send, slab_recv, end_send, end_recv, ready,
    ) = rest[views:]
    group_rows = rows // slabs
    d = lax.axis_index("depth")
    t = lax.axis_index("tile")
    bf16 = jnp.bfloat16
    LOW, HIGH = 0, 1
    colours = channels - 1

    renders = (d > 0) & (d < slabs - 1)
    has_outer = (d == 1) | (d == slabs - 2)
    between = (d > 1) & (d < slabs - 2)
    at_end = (d == 0) | (d == slabs - 1)
    outer_side = jnp.where(d == 1, LOW, HIGH)
    outer = jnp.where(d == 1, 0, slabs - 1)
    inner_side = 1 - outer_side
    inner = jnp.where(d == 1, 2, d - 1)
    step = jnp.where(2 * d < slabs, 1, slabs - 1)

    barrier = pltpu.get_barrier_semaphore()

    def signal(sem, peer):
        pl.semaphore_signal(sem, inc=1, device_id=peer, device_id_type=pl.DeviceIdType.MESH)

    @pl.when(d > 0)
    def _():
        signal(barrier, {"depth": d - 1})

    @pl.when(d < slabs - 1)
    def _():
        signal(barrier, {"depth": d + 1})

    @pl.when(t > 0)
    def _():
        signal(barrier, {"tile": t - 1})

    @pl.when(t < tiles - 1)
    def _():
        signal(barrier, {"tile": t + 1})

    sources = (density_in, pack_in, width_in, halo_in, height_in, depth_in)
    places = (density, pack_m, width_m, halo_m, height_m, depth_m)
    fetches = [
        pltpu.make_async_copy(src, dst, fetch_sem.at[i]) for i, (src, dst) in enumerate(zip(sources, places))
    ]
    smalls = [
        pltpu.make_async_copy(src, dst, small_sem.at[i])
        for i, (src, dst) in enumerate(zip((zoom_in, shift_in, weights_in, order_in), (zoom, shift, weights, order)))
    ]
    for fetch in smalls + fetches:
        fetch.start()

    def remote(src, dst, send, recv_sem, peer):
        return pltpu.make_async_remote_copy(
            src_ref=src, dst_ref=dst, send_sem=send, recv_sem=recv_sem,
            device_id=peer, device_id_type=pl.DeviceIdType.MESH,
        )

    to_left = remote(packed, from_right, tile_send.at[0], tile_recv.at[1], {"tile": t - 1})
    to_right = remote(packed, from_left, tile_send.at[1], tile_recv.at[0], {"tile": t + 1})

    pl.semaphore_wait(
        barrier,
        (d > 0).astype(jnp.int32) + (d < slabs - 1).astype(jnp.int32)
        + (t > 0).astype(jnp.int32) + (t < tiles - 1).astype(jnp.int32),
    )

    def pass_on(r):
        @pl.when((d > 0) & (d + r - 1 < slabs))
        def _():
            signal(ready.at[HIGH, r], {"depth": d - 1})

        @pl.when((d < slabs - 1) & (d - r + 1 >= 0))
        def _():
            signal(ready.at[LOW, r], {"depth": d + 1})

    def hear(r):
        @pl.when(d + r < slabs)
        def _():
            pl.semaphore_wait(ready.at[HIGH, r], 1)

        @pl.when(d - r >= 0)
        def _():
            pl.semaphore_wait(ready.at[LOW, r], 1)

    pass_on(2)

    cuts = [cells * c // CUTS_OF for c in CUTS] + [cells]
    parts = [slice(a, b) for a, b in zip(cuts, cuts[1:])]
    to_below = [
        remote(density_in.at[p], from_side.at[HIGH, p], depth_send.at[0, i], depth_recv.at[1, i], {"depth": d - 1})
        for i, p in enumerate(parts)
    ]
    to_above = [
        remote(density_in.at[p], from_side.at[LOW, p], depth_send.at[1, i], depth_recv.at[0, i], {"depth": d + 1})
        for i, p in enumerate(parts)
    ]

    @pl.when(d > 0)
    def _():
        to_below[0].start()

    @pl.when(d < slabs - 1)
    def _():
        to_above[0].start()

    fetches[0].wait()
    fetches[1].wait()
    whole = jnp.concatenate([density[z] for z in range(cells)], axis=1)
    packed[...] = matmul(whole, pack_m[...]).astype(bf16)

    @pl.when(t > 0)
    def _():
        to_left.start()

    @pl.when(t < tiles - 1)
    def _():
        to_right.start()

    @pl.when(t == 0)
    def _():
        from_left[...] = jnp.zeros_like(from_left)

    @pl.when(t == tiles - 1)
    def _():
        from_right[...] = jnp.zeros_like(from_right)

    @pl.when(d == 0)
    def _():
        from_side[LOW] = jnp.zeros((cells, rows, width), bf16)
        edges_side[LOW] = jnp.zeros((rows, width), bf16)

    @pl.when(d == slabs - 1)
    def _():
        from_side[HIGH] = jnp.zeros((cells, rows, width), bf16)
        edges_side[HIGH] = jnp.zeros((rows, width), bf16)

    for fetch in smalls:
        fetch.wait()

    pixel = lax.broadcasted_iota(jnp.int32, (rows, rows), 0).astype(jnp.float32)
    cell = lax.broadcasted_iota(jnp.int32, (rows, rows), 1).astype(jnp.float32)
    for v in range(views):
        where_at = zoom[v] * pixel + shift[v]
        table[v * rows : (v + 1) * rows] = jnp.maximum(0.0, 1.0 - jnp.abs(where_at - cell)).astype(bf16)

    def resample(plane, into, v, part):
        at = slice(0, views * rows) if v is None else slice(v * rows, (v + 1) * rows)
        for z in range(part.start, part.stop, 2):
            pair = matmul(table[at], jnp.concatenate([plane(z), plane(z + 1)], axis=1))
            into[z, at] = pair[:, :width]
            into[z + 1, at] = pair[:, width:]

    everything = slice(0, cells)
    resample(lambda z: density[z], sampled, None, everything)
    def blur_plane(block, sides, out, part):
        count = part.stop - part.start
        inside = matmul(block.reshape(count * rows, width), width_m[...])
        outside = matmul(sides, halo_m[:, part.start * width : part.stop * width])
        along_width = jnp.concatenate(
            [inside[z * rows : (z + 1) * rows] + outside[:, z * width : (z + 1) * width] for z in range(count)],
            axis=1,
        ).astype(bf16)
        flat = matmul(height_m[...], along_width).astype(bf16)
        for z in range(count):
            planes[out, part.start + z] = flat[:, z * width : (z + 1) * width]

    chunk = min(CHUNK, group_rows)
    per_group = group_rows // chunk
    extinction = -(EXTINCTION / (cells * slabs)) * LOG2E
    peak = basis - 1

    def coefficients(v, c):
        scale = extinction if c == colours else 1.0
        return [weights[v, c, k] * (math.exp(-0.5 * k * k) * scale) for k in range(basis)]

    def bumps(s, coefs):
        fall = jnp.exp2((-0.5 * peak * peak * LOG2E) * (s * s))
        ratio = jnp.exp2((peak * LOG2E) * s)
        sums = []
        for coef in coefs:
            total = coef[basis - 1] * ratio + coef[basis - 2]
            for k in range(basis - 3, -1, -1):
                total = total * ratio + coef[k]
            sums.append(total)
        return fall, sums

    tap = lax.broadcasted_iota(jnp.int32, (chunk, basis * chunk), 1)
    same = (tap % chunk == lax.broadcasted_iota(jnp.int32, (chunk, basis * chunk), 0)).astype(jnp.float32)
    for v in range(views):
        for c in range(channels):
            coef = coefficients(v, c)
            spread = jnp.zeros((chunk, basis * chunk), jnp.float32)
            for k in range(basis):
                spread = jnp.where(tap // chunk == k, coef[k], spread)
            spread = spread * same
            high = spread.astype(bf16)
            mixing[v, c * chunk : (c + 1) * chunk] = high
            mixing[v, (channels + c) * chunk : (channels + c + 1) * chunk] = (spread - high.astype(jnp.float32)).astype(bf16)

    def terms(s):
        ratio = jnp.exp2((peak * LOG2E) * s)
        each = [jnp.exp2((-0.5 * peak * peak * LOG2E) * (s * s))]
        for _ in range(1, basis):
            each.append(each[-1] * ratio)
        return jnp.concatenate([x.astype(bf16) for x in each], axis=0)

    def light(source, v, part, into, first, passing):
        for z in range(part.start, part.stop, 2):
            pair = [terms(source[y, pl.ds(v * rows + first, chunk), :]) for y in (z, z + 1)]
            mixed = matmul(mixing[v], jnp.concatenate(pair, axis=1))
            mixed = mixed[: channels * chunk] + mixed[channels * chunk :]
            for y in range(2):
                value = [
                    mixed[c * chunk : (c + 1) * chunk, y * width : (y + 1) * width] for c in range(channels)
                ]
                later = passing * jnp.exp2(value[colours])
                share = passing - later
                for c in range(colours):
                    into[v, c, z + y, pl.ds(first, chunk), :] = share * value[c]
                passing = later
        return passing

    def store_alpha(slab_index, v, i, value):
        group = i // per_group
        inside = pl.multiple_of((i % per_group) * chunk, chunk)
        alpha[slab_index, group, v, pl.ds(inside, chunk), :] = value.astype(bf16)

    def transfer(i, carry):
        first = pl.multiple_of(i * chunk, chunk)
        for v in range(views):
            passing = light(sampled, v, everything, lit, first, jnp.ones((chunk, width), jnp.float32))
            store_alpha(d, v, i, 1.0 - passing)
        return carry

    def send_part(i):
        @pl.when(d > 0)
        def _():
            to_below[i].start()

        @pl.when(d < slabs - 1)
        def _():
            to_above[i].start()

    middle = rows // chunk // 2
    lax.fori_loop(0, middle, transfer, 0, unroll=4)
    send_part(1)
    lax.fori_loop(middle, rows // chunk, transfer, 0, unroll=4)

    for fetch in fetches[2:]:
        fetch.wait()

    @pl.when(t > 0)
    def _():
        to_left.wait_send()
        to_right.wait_recv()

    @pl.when(t < tiles - 1)
    def _():
        to_right.wait_send()
        to_left.wait_recv()

    lane = lax.broadcasted_iota(jnp.int32, (rows, width), 1)
    edges[...] = jnp.where(
        lane < cells * RADIUS, from_right[...].astype(jnp.float32), from_left[...].astype(jnp.float32)
    ).astype(bf16)

    edges_below = remote(edges, edges_side.at[HIGH], edge_send.at[0], edge_recv.at[1], {"depth": d - 1})
    edges_above = remote(edges, edges_side.at[LOW], edge_send.at[1], edge_recv.at[0], {"depth": d + 1})

    @pl.when(d > 0)
    def _():
        edges_below.start()

    @pl.when(d < slabs - 1)
    def _():
        edges_above.start()

    send_part(2)
    blur_plane(density[...], edges[...], 1, everything)

    for r in range(2, slabs - 1):
        hear(r)
        if r < slabs - 2:
            pass_on(r + 1)

    def to_renderer(j):
        return remote(alpha.at[d], alpha.at[d], alpha_send.at[j], alpha_recv.at[d], {"depth": j})

    def beside_pair(s, j):
        pair = pl.ds(jnp.where(s == 0, 0, slabs - 2), 2)
        return remote(alpha.at[s, pair], alpha.at[s, pair], alpha_send.at[0], alpha_recv.at[s], {"depth": j})

    beyond = jnp.where((d == 1) | (d == 0), 3, 0)

    def to_end(i, end, near, across):
        which = (pl.ds(near, 1), pl.ds(across, 1), pl.ds(beyond, slabs - 3))[i]
        return remote(alpha.at[which, end], alpha.at[which, end], end_send.at[i], end_recv.at[i], {"depth": end})

    def tell_end(i):
        @pl.when(has_outer)
        def _():
            to_end(i, outer, d, inner).start()

    next_in = jnp.where(d == 0, 1, slabs - 2)

    def needs(j):
        return (j - d >= 2) | (d - j >= 2)

    outer_first = jnp.where(d == 1, 2 * group_rows, 0)

    def outer_chunk(part, i):
        first = pl.multiple_of(outer_first + i * chunk, chunk)
        at = pl.ds(first, chunk)
        for v in range(views):
            passing = jnp.ones((chunk, width), jnp.float32) if part.start == 0 else passing_outer[v, at, :]
            passing = light(sampled_outer, v, part, lit_outer, first, passing)
            if part.stop < cells:
                passing_outer[v, at, :] = passing
            else:
                store_alpha(outer, v, outer_first // chunk + i, 1.0 - passing)

    def inner_chunk(part, which, i):
        for v in range(views):
            at = slice(i * chunk, (i + 1) * chunk)
            coefs = [coefficients(v, colours)]
            power = jnp.zeros((chunk, width), jnp.float32) if part.start == 0 else power_inner[v, at, :]
            for z in range(part.start, part.stop):
                fall, sums = bumps(sampled_inner[z, v * rows + i * chunk : v * rows + (i + 1) * chunk, :], coefs)
                power = power + fall * sums[0]
            if part.stop < cells:
                power_inner[v, at, :] = power
            else:
                store_alpha(which, v, i, 1.0 - jnp.exp2(power))

    def take_inner(side, which, part):
        resample(lambda z: from_side[side, z], sampled_inner, None, part)
        for i in range(rows // chunk):
            inner_chunk(part, which, i)

    def take_sides(part):
        resample(lambda z: from_side[outer_side, z], sampled_outer, None, part)
        resample(lambda z: from_side[inner_side, z], sampled_inner, None, part)
        count, total = (slabs - 2) * per_group, rows // chunk
        for i in range(count):
            outer_chunk(part, i)
            for j in range(total * i // count, total * (i + 1) // count):
                inner_chunk(part, inner, j)

    for i, part in enumerate(parts):
        @pl.when(d > 0)
        def _():
            to_below[i].wait_send()
            to_above[i].wait_recv()
            if i == 1:
                edges_below.wait_send()
                edges_above.wait_recv()

        @pl.when(d < slabs - 1)
        def _():
            to_above[i].wait_send()
            to_below[i].wait_recv()
            if i == 1:
                edges_above.wait_send()
                edges_below.wait_recv()

        if i == 1:
            send_part(3)
        if i == 0:
            tell_end(0)
        if i == ALPHA_AT:
            for j in range(1, slabs - 1):
                @pl.when(needs(j))
                def _():
                    to_renderer(j).start()

            @pl.when(at_end)
            def _():
                beside_pair(d, next_in).start()

        if i:
            ready_part = slice(0, part.stop) if i == 1 else part
            blur_plane(from_side[LOW, ready_part], edges_side[LOW], 0, ready_part)
            blur_plane(from_side[HIGH, ready_part], edges_side[HIGH], 2, ready_part)

        @pl.when(has_outer)
        def _():
            take_sides(part)

    if slabs > 4:
        @pl.when(between)
        def _():
            take_inner(LOW, d - 1, everything)
            take_inner(HIGH, d + 1, everything)

    tell_end(1)

    gain = -OCCLUSION_GAIN * LOG2E / tap_total**3

    def occlusion(matrices, into):
        for g in range(0, rows, 2 * GROUP):
            def column(at):
                part = pl.ds(at, GROUP)
                return planes[:, :, part, :].reshape(3 * cells * GROUP, width)

            both = matmul(matrices, jnp.concatenate([column(g), column(g + GROUP)], axis=1))
            both = jnp.exp2(gain * both).astype(bf16)
            for i, block in enumerate(into):
                mine = both[i * cells * GROUP : (i + 1) * cells * GROUP]
                block[:, g : g + GROUP, :] = mine[:, :width].reshape(cells, GROUP, width)
                block[:, g + GROUP : g + 2 * GROUP, :] = mine[:, width:].reshape(cells, GROUP, width)

    @pl.when(has_outer)
    def _():
        occlusion(jnp.concatenate([depth_m[1], depth_m[2 * outer_side]], axis=0), [shade, shade_outer])

    @pl.when(at_end | between)
    def _():
        occlusion(depth_m[1], [shade])

    resample(lambda z: shade[z], sampled, None, everything)

    @pl.when(has_outer)
    def _():
        resample(lambda z: shade_outer[z], sampled_outer, None, everything)

    @pl.when(has_outer)
    def _():
        beside_pair(outer, outer).wait_recv()

    for s in range(slabs):
        far = (s - d >= 2) | (d - s >= 2)

        @pl.when(renders & far)
        def _():
            remote(alpha.at[s], alpha.at[s], alpha_send.at[0], alpha_recv.at[s], {"depth": s}).wait_recv()

    tell_end(2)

    def peer_of(k):
        return lax.rem(d + step * k, slabs)

    def slab_copy(v, k):
        return remote(
            slab.at[v, k], recv[v].at[d], slab_send.at[v, k], slab_recv.at[v, d], {"depth": peer_of(k)}
        )

    def slab_wait(v, s):
        remote(slab.at[v, 0], recv[v].at[s], slab_send.at[v, 0], slab_recv.at[v, s], {"depth": s}).wait_recv()

    def ahead(v, group, inside):
        passing = jnp.ones((chunk, width), jnp.float32)
        mine = jnp.zeros((chunk, width), jnp.float32)
        beside = jnp.zeros((chunk, width), jnp.float32)
        for q in range(slabs):
            slot = order[v, q]
            dense = alpha[slot, group, v, inside, :].astype(jnp.float32)
            mine = mine + (slot == d).astype(jnp.float32) * passing
            beside = beside + (slot == outer).astype(jnp.float32) * passing
            passing = passing * (1.0 - dense)
        return mine, beside, passing

    def gather(source, shaded, v, at):
        total = [jnp.zeros((chunk, width), jnp.float32)] * colours
        for z in range(cells):
            s = shaded[z, pl.ds(v * rows + at, chunk), :]
            total = [total[c] + source[v, c, z, pl.ds(at, chunk), :] * s for c in range(colours)]
        return total

    spans = [slice(i * chunk, (i + 1) * chunk) for i in range(per_group)]

    steps = sorted(range(1, slabs - 1), key=lambda k: abs(2 * k - slabs)) + [slabs - 1]
    for v in range(views):
        for k in steps + [0]:
            group = peer_of(k)
            start = pl.multiple_of(group * group_rows, group_rows)
            if k == 0:
                for inside in spans:
                    total = gather(lit, sampled, v, start + inside.start)
                    for c in range(colours):
                        own[v, c, inside, :] = total[c]
                continue

            def fill(with_outer):
                for inside in spans:
                    at = start + inside.start
                    mine, beside, _ = ahead(v, group, inside)
                    total = [mine * x for x in gather(lit, sampled, v, at)]
                    if with_outer and k < slabs - 1:
                        other = gather(lit_outer, sampled_outer, v, at)
                        total = [total[c] + beside * other[c] for c in range(colours)]
                    for c in range(colours):
                        slab[v, k, c, inside, :] = total[c].astype(bf16)

            @pl.when(has_outer)
            def _():
                fill(True)
                slab_copy(v, k).start()

            if slabs > 4:
                @pl.when(between)
                def _():
                    fill(False)
                    slab_copy(v, k).start()

            if k == 1:
                @pl.when(at_end)
                def _():
                    for inside in spans:
                        total = gather(lit, sampled, v, start + inside.start)
                        for c in range(colours):
                            slab[v, k, c, inside, :] = total[c].astype(bf16)
                    slab_copy(v, k).start()

    for j in range(1, slabs - 1):
        @pl.when(needs(j))
        def _():
            to_renderer(j).wait_send()

    @pl.when(has_outer)
    def _():
        for i in range(3):
            to_end(i, outer, d, inner).wait_send()

    @pl.when(at_end)
    def _():
        for i in range(3):
            to_end(i, d, next_in, jnp.where(d == 0, 2, slabs - 3)).wait_recv()

    @pl.when(at_end)
    def _():
        beside_pair(d, next_in).wait_send()

    for v in range(views):
        @pl.when(at_end | between)
        def _():
            for inside in spans:
                mine, _, passing = ahead(v, d, inside)
                for c in range(colours):
                    image[v, c, inside, :] = mine * own[v, c, inside, :]
                image[v, colours, inside, :] = 1.0 - passing

        @pl.when(has_outer)
        def _():
            slab_wait(v, outer)
            for inside in spans:
                mine, beside, passing = ahead(v, d, inside)
                for c in range(colours):
                    image[v, c, inside, :] = (
                        mine * own[v, c, inside, :] + beside * recv[v][outer, c, inside, :].astype(jnp.float32)
                    )
                image[v, colours, inside, :] = 1.0 - passing

    for v in range(views):
        for s in range(1, slabs - 1):
            @pl.when(d != s)
            def _():
                slab_wait(v, s)
                for c in range(colours):
                    image[v, c] = image[v, c] + recv[v][s, c].astype(jnp.float32)

    for v in range(views):
        for k in range(1, slabs):
            sends = renders | at_end if k == 1 else renders

            @pl.when(sends)
            def _():
                slab_copy(v, k).wait_send()


def local(slabs, tiles, density, view_zoom, view_shift, tf_weights, perm_order):
    cells, rows, width = density.shape
    views, channels, basis = tf_weights.shape
    group_rows = rows // slabs
    chunk = min(CHUNK, group_rows)
    matrices, tap_total = constants(cells, rows, width)
    hbm = pl.BlockSpec(memory_space=pltpu.HBM)
    bf16, f32 = jnp.bfloat16, jnp.float32
    block = pltpu.VMEM((cells, rows, width), bf16)
    edge = pltpu.VMEM((rows, width), bf16)
    samples = pltpu.VMEM((cells, views * rows, width), f32)
    emitted = pltpu.VMEM((views, channels - 1, cells, rows, width), f32)
    per_pixel = pltpu.VMEM((views, rows, width), f32)
    dma = pltpu.SemaphoreType.DMA
    operands = (density, view_zoom, view_shift, tf_weights, perm_order, *matrices)
    return pl.pallas_call(
        functools.partial(kernel, slabs, tiles, tap_total),
        out_shape=pltpu.VMEM((views, channels, group_rows, width), f32),
        in_specs=[hbm] * len(operands),
        out_specs=pl.BlockSpec(memory_space=pltpu.VMEM),
        scratch_shapes=[pltpu.SMEM(x.shape, x.dtype) for x in operands[1:5]]
        + [block]
        + [pltpu.VMEM(m.shape, bf16) for m in matrices]
        + [
            pltpu.VMEM((views * rows, rows), bf16),
            edge, edge, edge, edge, pltpu.VMEM((2, rows, width), bf16),
            pltpu.VMEM((3, cells, rows, width), bf16), pltpu.VMEM((2, cells, rows, width), bf16),
            samples, samples, samples, emitted, emitted, block, block,
            pltpu.VMEM((views, 2 * channels * chunk, basis * chunk), bf16),
            per_pixel, per_pixel,
            pltpu.VMEM((slabs, slabs, views, group_rows, width), bf16),
            pltpu.VMEM((views, slabs, channels - 1, group_rows, width), bf16),
            pltpu.VMEM((views, channels - 1, group_rows, width), f32),
        ]
        + [pltpu.VMEM((slabs, channels - 1, group_rows, width), bf16)] * views
        + [dma((4,)), dma((1 + len(matrices),)), dma((2,)), dma((2,)), dma((2, len(CUTS))), dma((2, len(CUTS))), dma((2,)), dma((2,))]
        + [dma((slabs,)), dma((slabs,))]
        + [dma((views, slabs)), dma((views, slabs)), dma((3,)), dma((3,))]
        + [pltpu.SemaphoreType.REGULAR((2, slabs))],
        compiler_params=pltpu.CompilerParams(
            collective_id=0, has_side_effects=True, vmem_limit_bytes=48 * 1024 * 1024
        ),
    )(*[pltpu.with_memory_space_constraint(x, pltpu.HBM) for x in operands])


def solution(mesh):
    placed = (P("depth", None, "tile"), P(), P(), P(), P())
    return jax.shard_map(
        functools.partial(local, mesh.shape["depth"], mesh.shape["tile"]),
        mesh=mesh, in_specs=placed, out_specs=P(None, None, "depth", "tile"), check_vma=False,
    )
```

```python
import functools
import math

import jax
import jax.numpy as jnp
import numpy as np
from jax import lax
from jax.experimental import pallas as pl
from jax.experimental.pallas import tpu as pltpu
from jax.sharding import PartitionSpec as P

RADIUS = 8
OCCLUSION_GAIN = 1.5
EXTINCTION = 0.5
LOG2E = math.log2(math.e)
GROUP = 16
CHUNK = 32
CUTS = (0, 2, 4, 6)
CUTS_OF = 8
ALPHA_AT = 2


def rounded_taps():
    offsets = np.arange(-RADIUS, RADIUS + 1, dtype=np.float64)
    taps = np.exp(-offsets * offsets / 72.0)
    taps = (taps / taps.sum()).astype(jnp.bfloat16).astype(np.float64)
    return taps, float(taps.sum())


def band(out_count, in_count, shift, taps):
    offset = np.arange(in_count)[None, :] + shift - np.arange(out_count)[:, None]
    inside = np.abs(offset) <= RADIUS
    return np.where(inside, taps[np.clip(offset + RADIUS, 0, 2 * RADIUS)], 0.0)


def constants(cells, rows, width):
    taps, total = rounded_taps()
    pack = np.zeros((cells, width, width), np.float32)
    low = np.zeros((width, cells, width))
    high = np.zeros((width, cells, width))
    half = cells * RADIUS
    from_low = band(width, RADIUS, -RADIUS, taps).T
    from_high = band(width, RADIUS, width, taps).T
    for z in range(cells):
        for j in range(RADIUS):
            pack[z, j, z * RADIUS + j] = 1.0
            pack[z, width - RADIUS + j, half + z * RADIUS + j] = 1.0
        low[half + z * RADIUS : half + (z + 1) * RADIUS, z] = from_low
        high[z * RADIUS : (z + 1) * RADIUS, z] = from_high
    halo = (low + high).reshape(width, cells * width)
    depth = np.stack([np.kron(band(cells, 3 * cells, -s * cells, taps), np.eye(GROUP)) for s in (0, 1, 2)])
    arrays = (
        pack.reshape(cells * width, width),
        band(width, width, 0, taps).T,
        halo,
        band(rows, rows, 0, taps),
        depth,
    )
    return [jnp.asarray(a.astype(jnp.bfloat16)) for a in arrays], total


def matmul(a, b):
    return jnp.dot(a, b, preferred_element_type=jnp.float32)


def kernel(
    slabs, tiles, tap_total,
    density_in, zoom_in, shift_in, weights_in, order_in, pack_in, width_in, halo_in, height_in, depth_in,
    image,
    zoom, shift, weights, order, density, pack_m, width_m, halo_m, height_m, depth_m,
    table, packed, from_left, from_right, edges, edges_side,
    planes, from_side, sampled, sampled_outer, sampled_inner, lit, lit_outer, shade, shade_outer,
    mixing, passing_outer, power_inner, alpha, slab, own, *rest,
):
    views, channels, basis = weights_in.shape
    cells, rows, width = density_in.shape
    recv = rest[:views]
    (
        small_sem, fetch_sem, tile_send, tile_recv, depth_send, depth_recv, edge_send, edge_recv,
        alpha_send, alpha_recv, slab_send, slab_recv, end_send, end_recv, ready,
    ) = rest[views:]
    group_rows = rows // slabs
    d = lax.axis_index("depth")
    t = lax.axis_index("tile")
    bf16 = jnp.bfloat16
    LOW, HIGH = 0, 1
    colours = channels - 1

    renders = (d > 0) & (d < slabs - 1)
    has_outer = (d == 1) | (d == slabs - 2)
    between = (d > 1) & (d < slabs - 2)
    at_end = (d == 0) | (d == slabs - 1)
    outer_side = jnp.where(d == 1, LOW, HIGH)
    outer = jnp.where(d == 1, 0, slabs - 1)
    inner_side = 1 - outer_side
    inner = jnp.where(d == 1, 2, d - 1)
    step = jnp.where(2 * d < slabs, 1, slabs - 1)

    barrier = pltpu.get_barrier_semaphore()

    def signal(sem, peer):
        pl.semaphore_signal(sem, inc=1, device_id=peer, device_id_type=pl.DeviceIdType.MESH)

    @pl.when(d > 0)
    def _():
        signal(barrier, {"depth": d - 1})

    @pl.when(d < slabs - 1)
    def _():
        signal(barrier, {"depth": d + 1})

    @pl.when(t > 0)
    def _():
        signal(barrier, {"tile": t - 1})

    @pl.when(t < tiles - 1)
    def _():
        signal(barrier, {"tile": t + 1})

    sources = (density_in, pack_in, width_in, halo_in, height_in, depth_in)
    places = (density, pack_m, width_m, halo_m, height_m, depth_m)
    fetches = [
        pltpu.make_async_copy(src, dst, fetch_sem.at[i]) for i, (src, dst) in enumerate(zip(sources, places))
    ]
    smalls = [
        pltpu.make_async_copy(src, dst, small_sem.at[i])
        for i, (src, dst) in enumerate(zip((zoom_in, shift_in, weights_in, order_in), (zoom, shift, weights, order)))
    ]
    for fetch in smalls + fetches:
        fetch.start()

    def remote(src, dst, send, recv_sem, peer):
        return pltpu.make_async_remote_copy(
            src_ref=src, dst_ref=dst, send_sem=send, recv_sem=recv_sem,
            device_id=peer, device_id_type=pl.DeviceIdType.MESH,
        )

    to_left = remote(packed, from_right, tile_send.at[0], tile_recv.at[1], {"tile": t - 1})
    to_right = remote(packed, from_left, tile_send.at[1], tile_recv.at[0], {"tile": t + 1})

    pl.semaphore_wait(
        barrier,
        (d > 0).astype(jnp.int32) + (d < slabs - 1).astype(jnp.int32)
        + (t > 0).astype(jnp.int32) + (t < tiles - 1).astype(jnp.int32),
    )

    def pass_on(r):
        @pl.when((d > 0) & (d + r - 1 < slabs))
        def _():
            signal(ready.at[HIGH, r], {"depth": d - 1})

        @pl.when((d < slabs - 1) & (d - r + 1 >= 0))
        def _():
            signal(ready.at[LOW, r], {"depth": d + 1})

    def hear(r):
        @pl.when(d + r < slabs)
        def _():
            pl.semaphore_wait(ready.at[HIGH, r], 1)

        @pl.when(d - r >= 0)
        def _():
            pl.semaphore_wait(ready.at[LOW, r], 1)

    pass_on(2)

    cuts = [cells * c // CUTS_OF for c in CUTS] + [cells]
    parts = [slice(a, b) for a, b in zip(cuts, cuts[1:])]
    to_below = [
        remote(density_in.at[p], from_side.at[HIGH, p], depth_send.at[0, i], depth_recv.at[1, i], {"depth": d - 1})
        for i, p in enumerate(parts)
    ]
    to_above = [
        remote(density_in.at[p], from_side.at[LOW, p], depth_send.at[1, i], depth_recv.at[0, i], {"depth": d + 1})
        for i, p in enumerate(parts)
    ]

    @pl.when(d > 0)
    def _():
        to_below[0].start()

    @pl.when(d < slabs - 1)
    def _():
        to_above[0].start()

    fetches[0].wait()
    fetches[1].wait()
    whole = jnp.concatenate([density[z] for z in range(cells)], axis=1)
    packed[...] = matmul(whole, pack_m[...]).astype(bf16)

    @pl.when(t > 0)
    def _():
        to_left.start()

    @pl.when(t < tiles - 1)
    def _():
        to_right.start()

    @pl.when(t == 0)
    def _():
        from_left[...] = jnp.zeros_like(from_left)

    @pl.when(t == tiles - 1)
    def _():
        from_right[...] = jnp.zeros_like(from_right)

    @pl.when(d == 0)
    def _():
        from_side[LOW] = jnp.zeros((cells, rows, width), bf16)
        edges_side[LOW] = jnp.zeros((rows, width), bf16)

    @pl.when(d == slabs - 1)
    def _():
        from_side[HIGH] = jnp.zeros((cells, rows, width), bf16)
        edges_side[HIGH] = jnp.zeros((rows, width), bf16)

    for fetch in smalls:
        fetch.wait()

    pixel = lax.broadcasted_iota(jnp.int32, (rows, rows), 0).astype(jnp.float32)
    cell = lax.broadcasted_iota(jnp.int32, (rows, rows), 1).astype(jnp.float32)
    for v in range(views):
        where_at = zoom[v] * pixel + shift[v]
        table[v * rows : (v + 1) * rows] = jnp.maximum(0.0, 1.0 - jnp.abs(where_at - cell)).astype(bf16)

    def resample(plane, into, v, part):
        at = slice(0, views * rows) if v is None else slice(v * rows, (v + 1) * rows)
        for z in range(part.start, part.stop, 2):
            pair = matmul(table[at], jnp.concatenate([plane(z), plane(z + 1)], axis=1))
            into[z, at] = pair[:, :width]
            into[z + 1, at] = pair[:, width:]

    everything = slice(0, cells)
    resample(lambda z: density[z], sampled, None, everything)
    def blur_plane(block, sides, out, part):
        count = part.stop - part.start
        inside = matmul(block.reshape(count * rows, width), width_m[...])
        outside = matmul(sides, halo_m[:, part.start * width : part.stop * width])
        along_width = jnp.concatenate(
            [inside[z * rows : (z + 1) * rows] + outside[:, z * width : (z + 1) * width] for z in range(count)],
            axis=1,
        ).astype(bf16)
        flat = matmul(height_m[...], along_width).astype(bf16)
        for z in range(count):
            planes[out, part.start + z] = flat[:, z * width : (z + 1) * width]

    chunk = min(CHUNK, group_rows)
    per_group = group_rows // chunk
    extinction = -(EXTINCTION / (cells * slabs)) * LOG2E
    peak = basis - 1

    def coefficients(v, c):
        scale = extinction if c == colours else 1.0
        return [weights[v, c, k] * (math.exp(-0.5 * k * k) * scale) for k in range(basis)]

    def bumps(s, coefs):
        fall = jnp.exp2((-0.5 * peak * peak * LOG2E) * (s * s))
        ratio = jnp.exp2((peak * LOG2E) * s)
        sums = []
        for coef in coefs:
            total = coef[basis - 1] * ratio + coef[basis - 2]
            for k in range(basis - 3, -1, -1):
                total = total * ratio + coef[k]
            sums.append(total)
        return fall, sums

    tap = lax.broadcasted_iota(jnp.int32, (chunk, basis * chunk), 1)
    same = (tap % chunk == lax.broadcasted_iota(jnp.int32, (chunk, basis * chunk), 0)).astype(jnp.float32)
    for v in range(views):
        for c in range(channels):
            coef = coefficients(v, c)
            spread = jnp.zeros((chunk, basis * chunk), jnp.float32)
            for k in range(basis):
                spread = jnp.where(tap // chunk == k, coef[k], spread)
            spread = spread * same
            high = spread.astype(bf16)
            mixing[v, c * chunk : (c + 1) * chunk] = high
            mixing[v, (channels + c) * chunk : (channels + c + 1) * chunk] = (spread - high.astype(jnp.float32)).astype(bf16)

    def terms(s):
        ratio = jnp.exp2((peak * LOG2E) * s)
        each = [jnp.exp2((-0.5 * peak * peak * LOG2E) * (s * s))]
        for _ in range(1, basis):
            each.append(each[-1] * ratio)
        return jnp.concatenate([x.astype(bf16) for x in each], axis=0)

    def light(source, v, part, into, first, passing):
        for z in range(part.start, part.stop, 2):
            pair = [terms(source[y, pl.ds(v * rows + first, chunk), :]) for y in (z, z + 1)]
            mixed = matmul(mixing[v], jnp.concatenate(pair, axis=1))
            mixed = mixed[: channels * chunk] + mixed[channels * chunk :]
            for y in range(2):
                value = [
                    mixed[c * chunk : (c + 1) * chunk, y * width : (y + 1) * width] for c in range(channels)
                ]
                later = passing * jnp.exp2(value[colours])
                share = passing - later
                for c in range(colours):
                    into[v, c, z + y, pl.ds(first, chunk), :] = share * value[c]
                passing = later
        return passing

    def store_alpha(slab_index, v, i, value):
        group = i // per_group
        inside = pl.multiple_of((i % per_group) * chunk, chunk)
        alpha[slab_index, group, v, pl.ds(inside, chunk), :] = value.astype(bf16)

    def transfer(i, carry):
        first = pl.multiple_of(i * chunk, chunk)
        for v in range(views):
            passing = light(sampled, v, everything, lit, first, jnp.ones((chunk, width), jnp.float32))
            store_alpha(d, v, i, 1.0 - passing)
        return carry

    def send_part(i):
        @pl.when(d > 0)
        def _():
            to_below[i].start()

        @pl.when(d < slabs - 1)
        def _():
            to_above[i].start()

    middle = rows // chunk // 2
    lax.fori_loop(0, middle, transfer, 0, unroll=4)
    send_part(1)
    lax.fori_loop(middle, rows // chunk, transfer, 0, unroll=4)

    for fetch in fetches[2:]:
        fetch.wait()

    @pl.when(t > 0)
    def _():
        to_left.wait_send()
        to_right.wait_recv()

    @pl.when(t < tiles - 1)
    def _():
        to_right.wait_send()
        to_left.wait_recv()

    lane = lax.broadcasted_iota(jnp.int32, (rows, width), 1)
    edges[...] = jnp.where(
        lane < cells * RADIUS, from_right[...].astype(jnp.float32), from_left[...].astype(jnp.float32)
    ).astype(bf16)

    edges_below = remote(edges, edges_side.at[HIGH], edge_send.at[0], edge_recv.at[1], {"depth": d - 1})
    edges_above = remote(edges, edges_side.at[LOW], edge_send.at[1], edge_recv.at[0], {"depth": d + 1})

    @pl.when(d > 0)
    def _():
        edges_below.start()

    @pl.when(d < slabs - 1)
    def _():
        edges_above.start()

    send_part(2)
    blur_plane(density[...], edges[...], 1, everything)

    for r in range(2, slabs - 1):
        hear(r)
        if r < slabs - 2:
            pass_on(r + 1)

    def to_renderer(j):
        return remote(alpha.at[d], alpha.at[d], alpha_send.at[j], alpha_recv.at[d], {"depth": j})

    def beside_pair(s, j):
        pair = pl.ds(jnp.where(s == 0, 0, slabs - 2), 2)
        return remote(alpha.at[s, pair], alpha.at[s, pair], alpha_send.at[0], alpha_recv.at[s], {"depth": j})

    beyond = jnp.where((d == 1) | (d == 0), 3, 0)

    def to_end(i, end, near, across):
        which = (pl.ds(near, 1), pl.ds(across, 1), pl.ds(beyond, slabs - 3))[i]
        return remote(alpha.at[which, end], alpha.at[which, end], end_send.at[i], end_recv.at[i], {"depth": end})

    def tell_end(i):
        @pl.when(has_outer)
        def _():
            to_end(i, outer, d, inner).start()

    next_in = jnp.where(d == 0, 1, slabs - 2)

    def needs(j):
        return (j - d >= 2) | (d - j >= 2)

    outer_first = jnp.where(d == 1, 2 * group_rows, 0)

    def outer_chunk(part, i):
        first = pl.multiple_of(outer_first + i * chunk, chunk)
        at = pl.ds(first, chunk)
        for v in range(views):
            passing = jnp.ones((chunk, width), jnp.float32) if part.start == 0 else passing_outer[v, at, :]
            passing = light(sampled_outer, v, part, lit_outer, first, passing)
            if part.stop < cells:
                passing_outer[v, at, :] = passing
            else:
                store_alpha(outer, v, outer_first // chunk + i, 1.0 - passing)

    def inner_chunk(part, which, i):
        for v in range(views):
            at = slice(i * chunk, (i + 1) * chunk)
            coefs = [coefficients(v, colours)]
            power = jnp.zeros((chunk, width), jnp.float32) if part.start == 0 else power_inner[v, at, :]
            for z in range(part.start, part.stop):
                fall, sums = bumps(sampled_inner[z, v * rows + i * chunk : v * rows + (i + 1) * chunk, :], coefs)
                power = power + fall * sums[0]
            if part.stop < cells:
                power_inner[v, at, :] = power
            else:
                store_alpha(which, v, i, 1.0 - jnp.exp2(power))

    def take_inner(side, which, part):
        resample(lambda z: from_side[side, z], sampled_inner, None, part)
        for i in range(rows // chunk):
            inner_chunk(part, which, i)

    def take_sides(part):
        resample(lambda z: from_side[outer_side, z], sampled_outer, None, part)
        resample(lambda z: from_side[inner_side, z], sampled_inner, None, part)
        count, total = (slabs - 2) * per_group, rows // chunk
        for i in range(count):
            outer_chunk(part, i)
            for j in range(total * i // count, total * (i + 1) // count):
                inner_chunk(part, inner, j)

    for i, part in enumerate(parts):
        @pl.when(d > 0)
        def _():
            to_below[i].wait_send()
            to_above[i].wait_recv()
            if i == 1:
                edges_below.wait_send()
                edges_above.wait_recv()

        @pl.when(d < slabs - 1)
        def _():
            to_above[i].wait_send()
            to_below[i].wait_recv()
            if i == 1:
                edges_above.wait_send()
                edges_below.wait_recv()

        if i == 1:
            send_part(3)
        if i == 0:
            tell_end(0)
        if i == ALPHA_AT:
            for j in range(1, slabs - 1):
                @pl.when(needs(j))
                def _():
                    to_renderer(j).start()

            @pl.when(at_end)
            def _():
                beside_pair(d, next_in).start()

        if i:
            ready_part = slice(0, part.stop) if i == 1 else part
            blur_plane(from_side[LOW, ready_part], edges_side[LOW], 0, ready_part)
            blur_plane(from_side[HIGH, ready_part], edges_side[HIGH], 2, ready_part)

        @pl.when(has_outer)
        def _():
            take_sides(part)

    if slabs > 4:
        @pl.when(between)
        def _():
            take_inner(LOW, d - 1, everything)
            take_inner(HIGH, d + 1, everything)

    tell_end(1)

    gain = -OCCLUSION_GAIN * LOG2E / tap_total**3

    def occlusion(matrices, into):
        for g in range(0, rows, 2 * GROUP):
            def column(at):
                part = pl.ds(at, GROUP)
                return planes[:, :, part, :].reshape(3 * cells * GROUP, width)

            both = matmul(matrices, jnp.concatenate([column(g), column(g + GROUP)], axis=1))
            both = jnp.exp2(gain * both).astype(bf16)
            for i, block in enumerate(into):
                mine = both[i * cells * GROUP : (i + 1) * cells * GROUP]
                block[:, g : g + GROUP, :] = mine[:, :width].reshape(cells, GROUP, width)
                block[:, g + GROUP : g + 2 * GROUP, :] = mine[:, width:].reshape(cells, GROUP, width)

    @pl.when(has_outer)
    def _():
        occlusion(jnp.concatenate([depth_m[1], depth_m[2 * outer_side]], axis=0), [shade, shade_outer])

    @pl.when(at_end | between)
    def _():
        occlusion(depth_m[1], [shade])

    resample(lambda z: shade[z], sampled, None, everything)

    @pl.when(has_outer)
    def _():
        resample(lambda z: shade_outer[z], sampled_outer, None, everything)

    @pl.when(has_outer)
    def _():
        beside_pair(outer, outer).wait_recv()

    for s in range(slabs):
        far = (s - d >= 2) | (d - s >= 2)

        @pl.when(renders & far)
        def _():
            remote(alpha.at[s], alpha.at[s], alpha_send.at[0], alpha_recv.at[s], {"depth": s}).wait_recv()

    tell_end(2)

    def peer_of(k):
        return lax.rem(d + step * k, slabs)

    def slab_copy(v, k):
        return remote(
            slab.at[v, k], recv[v].at[d], slab_send.at[v, k], slab_recv.at[v, d], {"depth": peer_of(k)}
        )

    def slab_wait(v, s):
        remote(slab.at[v, 0], recv[v].at[s], slab_send.at[v, 0], slab_recv.at[v, s], {"depth": s}).wait_recv()

    def ahead(v, group, inside):
        passing = jnp.ones((chunk, width), jnp.float32)
        mine = jnp.zeros((chunk, width), jnp.float32)
        beside = jnp.zeros((chunk, width), jnp.float32)
        for q in range(slabs):
            slot = order[v, q]
            dense = alpha[slot, group, v, inside, :].astype(jnp.float32)
            mine = mine + (slot == d).astype(jnp.float32) * passing
            beside = beside + (slot == outer).astype(jnp.float32) * passing
            passing = passing * (1.0 - dense)
        return mine, beside, passing

    def gather(source, shaded, v, at):
        total = [jnp.zeros((chunk, width), jnp.float32)] * colours
        for z in range(cells):
            s = shaded[z, pl.ds(v * rows + at, chunk), :]
            total = [total[c] + source[v, c, z, pl.ds(at, chunk), :] * s for c in range(colours)]
        return total

    spans = [slice(i * chunk, (i + 1) * chunk) for i in range(per_group)]

    steps = [slabs - 1] + sorted(range(1, slabs - 1), key=lambda k: abs(2 * k - slabs))
    for v in range(views):
        for k in steps + [0]:
            group = peer_of(k)
            start = pl.multiple_of(group * group_rows, group_rows)
            if k == 0:
                for inside in spans:
                    total = gather(lit, sampled, v, start + inside.start)
                    for c in range(colours):
                        own[v, c, inside, :] = total[c]
                continue

            def fill(with_outer):
                for inside in spans:
                    at = start + inside.start
                    mine, beside, _ = ahead(v, group, inside)
                    total = [mine * x for x in gather(lit, sampled, v, at)]
                    if with_outer and k < slabs - 1:
                        other = gather(lit_outer, sampled_outer, v, at)
                        total = [total[c] + beside * other[c] for c in range(colours)]
                    for c in range(colours):
                        slab[v, k, c, inside, :] = total[c].astype(bf16)

            @pl.when(has_outer)
            def _():
                fill(True)
                slab_copy(v, k).start()

            if slabs > 4:
                @pl.when(between)
                def _():
                    fill(False)
                    slab_copy(v, k).start()

            if k == 1:
                @pl.when(at_end)
                def _():
                    for inside in spans:
                        total = gather(lit, sampled, v, start + inside.start)
                        for c in range(colours):
                            slab[v, k, c, inside, :] = total[c].astype(bf16)
                    slab_copy(v, k).start()

    for j in range(1, slabs - 1):
        @pl.when(needs(j))
        def _():
            to_renderer(j).wait_send()

    @pl.when(has_outer)
    def _():
        for i in range(3):
            to_end(i, outer, d, inner).wait_send()

    @pl.when(at_end)
    def _():
        for i in range(3):
            to_end(i, d, next_in, jnp.where(d == 0, 2, slabs - 3)).wait_recv()

    @pl.when(at_end)
    def _():
        beside_pair(d, next_in).wait_send()

    for v in range(views):
        @pl.when(at_end | between)
        def _():
            for inside in spans:
                mine, _, passing = ahead(v, d, inside)
                for c in range(colours):
                    image[v, c, inside, :] = mine * own[v, c, inside, :]
                image[v, colours, inside, :] = 1.0 - passing

        @pl.when(has_outer)
        def _():
            slab_wait(v, outer)
            for inside in spans:
                mine, beside, passing = ahead(v, d, inside)
                for c in range(colours):
                    image[v, c, inside, :] = (
                        mine * own[v, c, inside, :] + beside * recv[v][outer, c, inside, :].astype(jnp.float32)
                    )
                image[v, colours, inside, :] = 1.0 - passing

    for v in range(views):
        for s in range(1, slabs - 1):
            @pl.when(d != s)
            def _():
                slab_wait(v, s)
                for c in range(colours):
                    image[v, c] = image[v, c] + recv[v][s, c].astype(jnp.float32)

    for v in range(views):
        for k in range(1, slabs):
            sends = renders | at_end if k == 1 else renders

            @pl.when(sends)
            def _():
                slab_copy(v, k).wait_send()


def local(slabs, tiles, density, view_zoom, view_shift, tf_weights, perm_order):
    cells, rows, width = density.shape
    views, channels, basis = tf_weights.shape
    group_rows = rows // slabs
    chunk = min(CHUNK, group_rows)
    matrices, tap_total = constants(cells, rows, width)
    hbm = pl.BlockSpec(memory_space=pltpu.HBM)
    bf16, f32 = jnp.bfloat16, jnp.float32
    block = pltpu.VMEM((cells, rows, width), bf16)
    edge = pltpu.VMEM((rows, width), bf16)
    samples = pltpu.VMEM((cells, views * rows, width), f32)
    emitted = pltpu.VMEM((views, channels - 1, cells, rows, width), f32)
    per_pixel = pltpu.VMEM((views, rows, width), f32)
    dma = pltpu.SemaphoreType.DMA
    operands = (density, view_zoom, view_shift, tf_weights, perm_order, *matrices)
    return pl.pallas_call(
        functools.partial(kernel, slabs, tiles, tap_total),
        out_shape=pltpu.VMEM((views, channels, group_rows, width), f32),
        in_specs=[hbm] * len(operands),
        out_specs=pl.BlockSpec(memory_space=pltpu.VMEM),
        scratch_shapes=[pltpu.SMEM(x.shape, x.dtype) for x in operands[1:5]]
        + [block]
        + [pltpu.VMEM(m.shape, bf16) for m in matrices]
        + [
            pltpu.VMEM((views * rows, rows), bf16),
            edge, edge, edge, edge, pltpu.VMEM((2, rows, width), bf16),
            pltpu.VMEM((3, cells, rows, width), bf16), pltpu.VMEM((2, cells, rows, width), bf16),
            samples, samples, samples, emitted, emitted, block, block,
            pltpu.VMEM((views, 2 * channels * chunk, basis * chunk), bf16),
            per_pixel, per_pixel,
            pltpu.VMEM((slabs, slabs, views, group_rows, width), bf16),
            pltpu.VMEM((views, slabs, channels - 1, group_rows, width), bf16),
            pltpu.VMEM((views, channels - 1, group_rows, width), f32),
        ]
        + [pltpu.VMEM((slabs, channels - 1, group_rows, width), bf16)] * views
        + [dma((4,)), dma((1 + len(matrices),)), dma((2,)), dma((2,)), dma((2, len(CUTS))), dma((2, len(CUTS))), dma((2,)), dma((2,))]
        + [dma((slabs,)), dma((slabs,))]
        + [dma((views, slabs)), dma((views, slabs)), dma((3,)), dma((3,))]
        + [pltpu.SemaphoreType.REGULAR((2, slabs))],
        compiler_params=pltpu.CompilerParams(
            collective_id=0, has_side_effects=True, vmem_limit_bytes=48 * 1024 * 1024
        ),
    )(*[pltpu.with_memory_space_constraint(x, pltpu.HBM) for x in operands])


def solution(mesh):
    placed = (P("depth", None, "tile"), P(), P(), P(), P())
    return jax.shard_map(
        functools.partial(local, mesh.shape["depth"], mesh.shape["tile"]),
        mesh=mesh, in_specs=placed, out_specs=P(None, None, "depth", "tile"), check_vma=False,
    )
```
